32 devices in a mesh: seq: 8 (over y, x, core), tp: 4 (over z).
Axes of the slice: x: 2, y: 2, z: 4, core: 2. Of those that a mesh axis runs over, the one named last changes fastest.
Arguments:
- layer_in: bfloat16 [2, 1024, 2048], P(None, 'seq'), may hold values from -6 to 6
- positions: int32 [2, 1024], P(None, 'seq'), may hold values from 0 to 4092, as said below
- first_gain: float32 [2048], replicated, may hold values from 0.5 to 1.5
- query_proj: bfloat16 [2048, 2048], P('seq', 'tp'), may hold values from -0.125 to 0.125
- key_projection: bfloat16 [2048, 1024], P('seq', 'tp'), may hold values from -0.125 to 0.125
- value_projection: bfloat16 [2048, 1024], P('seq', 'tp'), may hold values from -0.125 to 0.125
- gate_proj: bfloat16 [2048, 2048], P('seq', 'tp'), may hold values from -0.125 to 0.125
- output_proj: bfloat16 [2048, 2048], P('tp', 'seq'), may hold values from -1.5 to 1.5
- query_gain: float32 [128], replicated, may hold values from 0.5 to 1.5
- key_norm_gain: float32 [128], replicated, may hold values from 0.5 to 1.5
- second_gain: float32 [2048], replicated, may hold values from 0.5 to 1.5
- hidden_gate: bfloat16 [2048, 6144], P('tp', 'seq'), may hold values from -0.125 to 0.125
- hidden_up: bfloat16 [2048, 6144], P('tp', 'seq'), may hold values from -0.125 to 0.125
- hidden_down: bfloat16 [6144, 2048], P('seq', 'tp'), may hold values from -0.078125 to 0.078125
- out_cotangent: bfloat16 [2, 1024, 2048], P(None, ('seq', 'tp')), may hold values from -6 to 6
Outputs:
- layer_out: bfloat16 [2, 1024, 2048], P(None, ('seq', 'tp'))
- input_grad: float32 [2, 1024, 2048], P(None, ('seq', 'tp'))
- grad_firstgain: float32 [2048], replicated
- grad_query: float32 [2048, 2048], P('seq', 'tp')
- grad_keyproj: float32 [2048, 1024], P('seq', 'tp')
- grad_valueproj: float32 [2048, 1024], P('seq', 'tp')
- grad_gating: float32 [2048, 2048], P('seq', 'tp')
- grad_outproj: float32 [2048, 2048], P('tp', 'seq')
- grad_qgain: float32 [128], replicated
- grad_kgain: float32 [128], replicated
- grad_secondgain: float32 [2048], replicated
- grad_hgate: float32 [2048, 6144], P('tp', 'seq')
- grad_hup: float32 [2048, 6144], P('tp', 'seq')
- grad_hdown: float32 [6144, 2048], P('seq', 'tp')
The draws below stay inside these ranges and needn't reach their ends.
Inputs may be any that keep to these rules, and one draw needn't show every extreme that they name: Within each micro-batch the first token has position 0, positions rise strictly from token to token, and the last token's position is 4092.
All inputs are finite; a program needn't handle non-finite values.
Results may differ from the reference program's by a relative error of at most 0.023.
Values may be sent and summed in bfloat16 or wider, within the bound.
No kernel may reach another device: no remote copies, remote signals or barrier semaphores. Data moves between devices by JAX's collectives and lax.ppermute only.
A program may use at most 192 MiB of HBM per device.

```python
import jax
import jax.numpy as jnp
from jax import lax

MODEL_DIM = 2048
QUERY_HEADS = 16
KEY_VALUE_HEADS = 8
HEAD_DIM = 128
FF = 6144
MICRO = 2
SEQUENCE_LENGTH = 1024


def draw_positions(key, part):
    steps = jax.random.randint(key, (MICRO, SEQUENCE_LENGTH), 1, 5, dtype=jnp.int32)
    places = jnp.arange(SEQUENCE_LENGTH, dtype=jnp.int32)[None, :]
    steps = jnp.where(places == 0, jnp.zeros_like(steps), steps)
    totals = jnp.cumsum(steps, axis=1, dtype=jnp.int32)
    last_value = jnp.full_like(totals, 4 * (SEQUENCE_LENGTH - 1))
    return jnp.where(places == SEQUENCE_LENGTH - 1, last_value, totals).astype(jnp.int32)


def level_of(key, extent, shards, least, largest):
    factor_of = 1.0
    for position, shards_of in shards:
        draws = jax.random.uniform(jax.random.fold_in(jax.random.fold_in(key, 6), position), (shards_of,), jnp.float32, least / len(shards), largest / len(shards))
        factor_of = factor_of * jnp.repeat(jnp.exp(draws), extent[position] // shards_of).reshape((-1,) + (1,) * (len(extent) - 1 - position))
    return factor_of


def scatter_about(key, extent, scale, reach, pieces=(), held_as=jnp.bfloat16):
    level = level_of(key, extent, pieces, -0.22, 0.18) if pieces else 1.0
    values = jax.random.normal(key, extent, jnp.float32) * scale * level
    return jnp.minimum(jnp.maximum(values, -reach), reach).astype(held_as)


def setup_inputs(seed: int = 0) -> dict:
    keys = jax.random.split(jax.random.key(seed), 16)
    layer_in = scatter_about(keys[0], (MICRO, SEQUENCE_LENGTH, MODEL_DIM), 1.0, 6.0, ((1, 8),))
    positions = draw_positions(jax.random.fold_in(keys[15], 71), 0)
    first_gain = jnp.clip(1.0 + 0.1 * jax.random.normal(keys[2], (MODEL_DIM,), jnp.float32), 0.5, 1.5)
    query_proj = scatter_about(keys[3], (MODEL_DIM, QUERY_HEADS * HEAD_DIM), MODEL_DIM ** -0.5, 0.125, ((0, 8), (1, 4)))
    key_projection = scatter_about(keys[4], (MODEL_DIM, KEY_VALUE_HEADS * HEAD_DIM), MODEL_DIM ** -0.5, 0.125, ((0, 8), (1, 4)))
    value_projection = scatter_about(keys[5], (MODEL_DIM, KEY_VALUE_HEADS * HEAD_DIM), MODEL_DIM ** -0.5, 0.125, ((0, 8), (1, 4)))
    gate_proj = scatter_about(keys[6], (MODEL_DIM, QUERY_HEADS * HEAD_DIM), MODEL_DIM ** -0.5, 0.125, ((0, 8), (1, 4)))
    output_proj = scatter_about(keys[7], (QUERY_HEADS * HEAD_DIM, MODEL_DIM), (HEAD_DIM // 8) ** -0.5, 1.5, ((0, 4), (1, 8)))
    query_gain = jnp.clip(1.0 + 0.1 * jax.random.normal(keys[8], (HEAD_DIM,), jnp.float32), 0.5, 1.5)
    key_norm_gain = jnp.clip(1.0 + 0.1 * jax.random.normal(keys[9], (HEAD_DIM,), jnp.float32), 0.5, 1.5)
    second_gain = jnp.clip(1.0 + 0.1 * jax.random.normal(keys[10], (MODEL_DIM,), jnp.float32), 0.5, 1.5)
    hidden_gate = scatter_about(keys[11], (MODEL_DIM, FF), MODEL_DIM ** -0.5, 0.125, ((0, 4), (1, 8)))
    hidden_up = scatter_about(keys[12], (MODEL_DIM, FF), MODEL_DIM ** -0.5, 0.125, ((0, 4), (1, 8)))
    hidden_down = scatter_about(keys[13], (FF, MODEL_DIM), FF ** -0.5, 0.078125, ((0, 8), (1, 4)))
    out_cotangent = scatter_about(keys[14], (MICRO, SEQUENCE_LENGTH, MODEL_DIM), 1.0, 6.0, ((1, 32),))
    return dict(layer_in=layer_in, positions=positions, first_gain=first_gain, query_proj=query_proj, key_projection=key_projection, value_projection=value_projection, gate_proj=gate_proj, output_proj=output_proj, query_gain=query_gain, key_norm_gain=key_norm_gain, second_gain=second_gain, hidden_gate=hidden_gate, hidden_up=hidden_up, hidden_down=hidden_down, out_cotangent=out_cotangent)


@jax.custom_vjp
def low(v):
    return lax.optimization_barrier(v.astype(jnp.bfloat16)).astype(jnp.float32)

@jax.custom_vjp
def low_back(v):
    return v

def low_keep(v):
    return (low(v), None)

def low_pass(kept, grad):
    return (grad,)

def back_keep(v):
    return (v, None)

def back_low(kept, grad):
    return (low(grad),)
low.defvjp(low_keep, low_pass)
low_back.defvjp(back_keep, back_low)
EPS = 1e-06
ROPE_BASE = 5000000.0
NEG_LARGE = -1e+30
HIGH = lax.Precision.HIGHEST

def matmul(left, right):
    return jnp.dot(left, right, precision=HIGH, preferred_element_type=jnp.float32)

def root_mean_square_scale(values, gain):
    return values * lax.rsqrt(lax.optimization_barrier(jnp.mean(values * values, axis=-1, keepdims=True)) + EPS) * gain

def rotate_half(values):
    middle = values.shape[-1] // 2
    return jnp.concatenate([-values[..., middle:], values[..., :middle]], axis=-1)

def rope_tables(places, head_width):
    middle = head_width // 2
    inverse = jnp.exp(-(jnp.arange(middle, dtype=jnp.float32) * 2.0 / head_width) * jnp.log(ROPE_BASE))
    angles = places.astype(jnp.float32)[:, None] * inverse[None, :]
    cosine_table = jnp.concatenate([jnp.cos(angles), jnp.cos(angles)], axis=-1)[:, None, :]
    sine_table = jnp.concatenate([jnp.sin(angles), jnp.sin(angles)], axis=-1)[:, None, :]
    return (cosine_table, sine_table)

def apply_rotary_embedding(values, cosine_table, sine_table):
    return values * cosine_table + rotate_half(values) * sine_table

def attention_layer(query_tensor, key_token_rows, value_token_rows):
    query_group_size = QUERY_HEADS // KEY_VALUE_HEADS
    keys_wide = jnp.repeat(key_token_rows, query_group_size, axis=1)
    values_wide = jnp.repeat(value_token_rows, query_group_size, axis=1)
    block_len = min(512, SEQUENCE_LENGTH)
    block_count = SEQUENCE_LENGTH // block_len
    query_blocks = query_tensor.reshape(block_count, block_len, QUERY_HEADS, HEAD_DIM)
    starts = jnp.arange(block_count, dtype=jnp.int32) * block_len
    key_pos = jnp.arange(SEQUENCE_LENGTH, dtype=jnp.int32)
    score_scale = HEAD_DIM ** (-0.5)

    def block_fn(block_item):
        query_rows, row_start = block_item
        scores = jnp.einsum('ihd,jhd->hij', query_rows, keys_wide, precision=HIGH) * score_scale
        scores = low_back(scores)
        allowed = key_pos[None, :] <= (row_start + jnp.arange(block_len, dtype=jnp.int32))[:, None]
        scores = jnp.where(allowed[None], scores, NEG_LARGE)
        probability = low(jax.nn.softmax(scores, axis=-1))
        return jnp.einsum('hij,jhd->ihd', probability, values_wide, precision=HIGH)
    result = lax.map(jax.checkpoint(block_fn), (query_blocks, starts))
    return result.reshape(SEQUENCE_LENGTH, QUERY_HEADS * HEAD_DIM)

def layer(layer_rows, first_gain, query_proj, key_projection, value_projection, gate_proj, output_proj, query_gain, key_norm_gain, second_gain, hidden_gate, hidden_up, hidden_down, cosine_table, sine_table):
    normed = low(root_mean_square_scale(layer_rows, first_gain))
    query_pre = low_back(matmul(normed, query_proj))
    key_before_norm = low_back(matmul(normed, key_projection))
    value_token_rows = low_back(low(matmul(normed, value_projection)))
    gate_pre = low_back(matmul(normed, gate_proj))
    query_tensor = low(apply_rotary_embedding(root_mean_square_scale(query_pre.reshape(SEQUENCE_LENGTH, QUERY_HEADS, HEAD_DIM), query_gain), cosine_table, sine_table))
    key_token_rows = low(apply_rotary_embedding(root_mean_square_scale(key_before_norm.reshape(SEQUENCE_LENGTH, KEY_VALUE_HEADS, HEAD_DIM), key_norm_gain), cosine_table, sine_table))
    attended_values = low_back(attention_layer(query_tensor, key_token_rows, value_token_rows.reshape(SEQUENCE_LENGTH, KEY_VALUE_HEADS, HEAD_DIM)))
    gated = low(attended_values * jax.nn.sigmoid(gate_pre))
    middle = layer_rows + low_back(matmul(gated, output_proj))
    normed_two = low(root_mean_square_scale(middle, second_gain))
    gate_act = low_back(matmul(normed_two, hidden_gate))
    upward = low_back(matmul(normed_two, hidden_up))
    hidden = low(jax.nn.silu(gate_act) * upward)
    return middle + low_back(matmul(hidden, hidden_down))

def reference(layer_in, positions, first_gain, query_proj, key_projection, value_projection, gate_proj, output_proj, query_gain, key_norm_gain, second_gain, hidden_gate, hidden_up, hidden_down, out_cotangent):
    weights = tuple((weight.astype(jnp.float32) for weight in (first_gain, query_proj, key_projection, value_projection, gate_proj, output_proj, query_gain, key_norm_gain, second_gain, hidden_gate, hidden_up, hidden_down)))

    def one_batch(totals, batch_item):
        batch_rows, places, cotangent = batch_item
        cosine_table, sine_table = rope_tables(places, HEAD_DIM)

        def forward(layer_rows, *params):
            return layer(layer_rows, *params, cosine_table, sine_table)
        result, pull = jax.vjp(forward, batch_rows.astype(jnp.float32), *weights)
        grads = pull(cotangent.astype(jnp.float32))
        totals = tuple((total + grad for total, grad in zip(totals, grads[1:])))
        return (totals, (result.astype(jnp.bfloat16), grads[0]))
    initial = tuple((jnp.zeros_like(weight) for weight in weights))
    sums, (outputs, input_grads) = lax.scan(one_batch, initial, (layer_in, positions, out_cotangent))
    return (outputs, input_grads, sums[0], sums[1], sums[2], sums[3], sums[4], sums[5], sums[6], sums[7], sums[8], sums[9], sums[10], sums[11])
```

```python
import jax
import jax.numpy as jnp
from jax import lax
from jax.sharding import PartitionSpec as P

EPS = 1e-06
ROPE_BASE = 5000000.0
NEG_LARGE = -1e30
F32 = jnp.float32
LOW = jnp.bfloat16


def root_mean_square_scale(values, gain):
    return values * lax.rsqrt(jnp.mean(values * values, axis=-1, keepdims=True) + EPS) * gain


def rotate_half(values):
    middle = values.shape[-1] // 2
    return jnp.concatenate([-values[..., middle:], values[..., :middle]], axis=-1)


def rope_tables(places, head_width):
    middle = head_width // 2
    inverse = jnp.exp(-(jnp.arange(middle, dtype=F32) * 2.0 / head_width) * jnp.log(ROPE_BASE))
    angles = places.astype(F32)[:, None] * inverse[None, :]
    cosine_table = jnp.concatenate([jnp.cos(angles), jnp.cos(angles)], axis=-1)[:, None, :]
    sine_table = jnp.concatenate([jnp.sin(angles), jnp.sin(angles)], axis=-1)[:, None, :]
    return (cosine_table, sine_table)


def apply_rotary_embedding(values, cosine_table, sine_table):
    return values * cosine_table + rotate_half(values) * sine_table


def dot_nn(left, right):
    return jnp.dot(left, right, preferred_element_type=F32)


def dot_nt(left, right):
    return lax.dot_general(left, right, (((1,), (1,)), ((), ())), preferred_element_type=F32)


def dot_tn(left, right):
    return lax.dot_general(left, right, (((0,), (0,)), ((), ())), preferred_element_type=F32)


def swap(value, axis, mask):
    count = lax.axis_size(axis)
    return lax.ppermute(value, axis, [(i, i ^ mask) for i in range(count)])


def gather_slots(value, axis, order):
    have = {0: value}
    for mask in order:
        have.update({s ^ mask: swap(v, axis, mask) for s, v in have.items()})
    return [have[s] for s in range(len(have))]


def scatter_slots(pieces, axis, order):
    now = dict(enumerate(pieces))
    for mask in order:
        now = {
            s: v.astype(F32) + swap(now[s ^ mask].astype(LOW), axis, mask).astype(F32)
            for s, v in now.items()
            if not s & mask
        }
    return now[0]


def spread_tp(value):
    count = lax.axis_size("tp")
    return [value] + [swap(value, "tp", k) for k in range(1, count)]


def tree_sum(terms):
    while len(terms) > 1:
        terms = [terms[i] + terms[i + 1] for i in range(0, len(terms), 2)]
    return terms[0]


def collect_tp(rows):
    count = lax.axis_size("tp")
    blocks = rows.reshape(count, rows.shape[0] // count, rows.shape[1])
    got = [blocks[0]]
    got += [swap(blocks[k].astype(LOW), "tp", k).astype(F32) for k in range(1, count)]
    return tree_sum(got)


def per_device(
    layer_in,
    positions,
    first_gain,
    query_proj,
    key_projection,
    value_projection,
    gate_proj,
    output_proj,
    query_gain,
    key_norm_gain,
    second_gain,
    hidden_gate,
    hidden_up,
    hidden_down,
    out_cotangent,
):
    micros, local_rows, width = layer_in.shape
    head = query_gain.shape[0]
    n = lax.axis_size("seq")
    p = lax.axis_size("tp")
    me_seq = lax.axis_index("seq")
    me_tp = lax.axis_index("tp")
    part = local_rows // p
    tokens = micros * local_rows
    ptok = micros * part
    block = width // n
    chunk = width // p
    q_width = query_proj.shape[1]
    kv_width = key_projection.shape[1]
    q_heads = q_width // head
    kv_heads = kv_width // head
    group = q_heads // kv_heads
    units = hidden_down.shape[0] // p
    total_rows = local_rows * n
    scale = head ** (-0.5)
    masks = [1 << b for b in range((n - 1).bit_length())]
    go_a = masks[1:] + masks[:1]
    go_b = masks[:0:-1] + masks[:1]
    back_a = masks[:1] + masks[1:]
    back_b = masks[:1] + masks[:0:-1]

    def permute_columns(value):
        return jnp.concatenate(
            [
                lax.dynamic_slice_in_dim(value, (me_seq ^ j) * block, block, value.ndim - 1)
                for j in range(n)
            ],
            axis=-1,
        )

    def token_slots(value):
        return jnp.stack(
            [lax.dynamic_slice_in_dim(value, (me_tp ^ k) * part, part, 1) for k in range(p)]
        )

    w_q = gather_slots(query_proj, "seq", go_a)
    w_kv = gather_slots(
        jnp.concatenate([key_projection, value_projection], axis=1), "seq", go_b
    )
    w_g = gather_slots(gate_proj, "seq", go_a)
    w_o = gather_slots(output_proj.T, "seq", go_b)

    def fetch_units(weight):
        blocks = weight.reshape(p, units, chunk)
        result = jnp.zeros((units, width), LOW)
        for k in range(p):
            piece = lax.dynamic_index_in_dim(blocks, me_tp ^ k, 0, keepdims=False)
            if k:
                piece = swap(piece, "tp", k)
            result = lax.dynamic_update_slice_in_dim(result, piece, (me_tp ^ k) * chunk, 1)
        return result

    half = units // 2
    f_gate = gather_slots(fetch_units(hidden_gate.T), "seq", go_a)
    f_up = gather_slots(fetch_units(hidden_up.T), "seq", go_b)
    down_own = fetch_units(hidden_down)
    f_down_a = gather_slots(down_own[:half], "seq", go_a)
    f_down_b = gather_slots(down_own[half:], "seq", go_b)
    f_gate = jnp.concatenate(f_gate)
    f_up = jnp.concatenate(f_up)
    f_down = jnp.concatenate([v for pair in zip(f_down_a, f_down_b) for v in pair])

    cot_part = out_cotangent.reshape(ptok, width)
    cot = jnp.concatenate(spread_tp(cot_part))

    x_slots = token_slots(layer_in)
    x_part = x_slots[0].reshape(ptok, width).astype(F32)
    x_perm = permute_columns(x_slots.reshape(tokens, width)).astype(F32)
    places = token_slots(positions).reshape(tokens)
    gain_perm = permute_columns(first_gain)
    cosine_table, sine_table = rope_tables(places, head)
    normed = root_mean_square_scale(x_perm, gain_perm).astype(LOW)
    w_q = jnp.concatenate(w_q)
    w_kv = jnp.concatenate(w_kv)
    w_g = jnp.concatenate(w_g)
    w_o = jnp.concatenate(w_o)
    query_pre = dot_nn(normed, w_q)
    kv_pre = dot_nn(normed, w_kv)
    key_pre = kv_pre[:, :kv_width]
    value_low = kv_pre[:, kv_width:].astype(LOW)
    gate_pre = dot_nn(normed, w_g)

    def shape_heads(query_in, key_in, query_scale, key_scale):
        query_out = apply_rotary_embedding(
            root_mean_square_scale(query_in.reshape(tokens, q_heads, head), query_scale),
            cosine_table,
            sine_table,
        )
        key_out = apply_rotary_embedding(
            root_mean_square_scale(key_in.reshape(tokens, kv_heads, head), key_scale),
            cosine_table,
            sine_table,
        )
        return (query_out, key_out)

    (query_rot, key_rot), heads_pull = jax.vjp(
        shape_heads, query_pre, key_pre, query_gain, key_norm_gain
    )

    def to_heads(value):
        return (
            value.reshape(p, micros, part, kv_heads, group, head)
            .transpose(1, 3, 4, 0, 2, 5)
            .reshape(micros, kv_heads, group, local_rows, head)
        )

    def from_heads(value):
        return (
            value.reshape(micros, kv_heads, group, p, part, head)
            .transpose(3, 0, 4, 1, 2, 5)
            .reshape(tokens, q_width)
        )

    query_low = to_heads(query_rot.astype(LOW))
    key_low = key_rot.astype(LOW).reshape(tokens, kv_width)

    def all_keys(slots):
        return (
            jnp.stack(slots)
            .reshape(n, p, micros, part, kv_heads, head)
            .transpose(2, 4, 0, 1, 3, 5)
            .reshape(micros, kv_heads, total_rows, head)
        )

    key_all = all_keys(gather_slots(key_low, "seq", go_a))
    value_all = all_keys(gather_slots(value_low, "seq", go_b))
    inside = jnp.concatenate(
        [(me_tp ^ k) * part + jnp.arange(part, dtype=jnp.int32) for k in range(p)]
    )
    query_pos = me_seq * local_rows + inside
    key_pos = jnp.concatenate([(me_seq ^ j) * local_rows + inside for j in range(n)])
    allowed = key_pos[None, :] <= query_pos[:, None]

    def all_scores():
        scores = (
            jnp.einsum("mngid,mnjd->mngij", query_low, key_all, preferred_element_type=F32) * scale
        )
        return jnp.where(allowed, scores, NEG_LARGE)

    scores = all_scores()
    peak = jnp.max(scores, axis=-1, keepdims=True)
    weights = jnp.exp(scores - peak)
    probability = weights / jnp.sum(weights, axis=-1, keepdims=True)
    probs_low = probability.astype(LOW)
    attended_heads = jnp.einsum("mngij,mnjd->mngid", probs_low, value_all, preferred_element_type=F32)
    attended = from_heads(attended_heads)
    gate_sig = jax.nn.sigmoid(gate_pre)
    gated_low = (attended * gate_sig).astype(LOW)
    branch = permute_columns(collect_tp(dot_nt(gated_low, w_o)))
    middle = x_part + branch
    normed_two = root_mean_square_scale(middle, second_gain).astype(LOW)
    n2 = jnp.concatenate(spread_tp(normed_two))

    gate_act = dot_nt(f_gate, n2)
    upward = dot_nt(f_up, n2)
    hidden_grad = dot_nt(f_down, cot)
    sig = jax.nn.sigmoid(gate_act)
    silu = gate_act * sig
    hidden_low = (silu * upward).astype(LOW)
    gate_grad = (hidden_grad * upward * sig * (1.0 + gate_act * (1.0 - sig))).astype(LOW)
    upward_grad = (hidden_grad * silu).astype(LOW)
    normed_two_grad = collect_tp(dot_tn(gate_grad, f_gate) + dot_tn(upward_grad, f_up))
    ffn_out = collect_tp(dot_tn(hidden_low, f_down))
    layer_rows = (middle + ffn_out).astype(LOW)
    d_gate = dot_nn(gate_grad, n2).astype(LOW).reshape(n, units, width)
    d_up = dot_nn(upward_grad, n2).astype(LOW).reshape(n, units, width)
    d_down = dot_nn(hidden_low, cot).astype(LOW).reshape(n, units, width)

    def return_units(own):
        result = jnp.zeros((p, units, chunk), F32)
        for k in range(p):
            piece = lax.dynamic_slice_in_dim(own, (me_tp ^ k) * chunk, chunk, 1)
            if k:
                piece = swap(piece.astype(LOW), "tp", k).astype(F32)
            result = lax.dynamic_update_slice_in_dim(result, piece[None], me_tp ^ k, 0)
        return result.reshape(p * units, chunk)

    grad_hgate = return_units(scatter_slots(list(d_gate), "seq", back_a)).T
    grad_hup = return_units(scatter_slots(list(d_up), "seq", back_b)).T
    grad_hdown = return_units(
        jnp.concatenate(
            [
                scatter_slots(list(d_down[:, :half]), "seq", back_a),
                scatter_slots(list(d_down[:, half:]), "seq", back_b),
            ]
        )
    )

    norm_two_pull = jax.vjp(root_mean_square_scale, middle, second_gain)[1]
    middle_from, grad_second = norm_two_pull(normed_two_grad)
    middle_grad = cot_part.astype(F32) + middle_from
    branch_grad = jnp.concatenate(spread_tp(permute_columns(middle_grad.astype(LOW))))
    gated_grad = dot_nn(branch_grad, w_o)
    attended_grad = (gated_grad * gate_sig).astype(LOW)
    gate_pre_grad = (gated_grad * attended * gate_sig * (1.0 - gate_sig)).astype(LOW)
    attended_grad_heads = to_heads(attended_grad)
    delta = jnp.sum(attended_grad_heads.astype(F32) * attended_heads, axis=-1, keepdims=True)
    probs_grad = jnp.einsum(
        "mngid,mnjd->mngij", attended_grad_heads, value_all, preferred_element_type=F32
    )
    scores_grad = (probability * (probs_grad - delta)).astype(LOW)
    query_grad = from_heads(
        jnp.einsum("mngij,mnjd->mngid", scores_grad, key_all, preferred_element_type=F32)
    )
    key_piece = jnp.einsum("mngij,mngid->mnjd", scores_grad, query_low, preferred_element_type=F32)
    value_piece = jnp.einsum(
        "mngij,mngid->mnjd", probs_low, attended_grad_heads, preferred_element_type=F32
    )

    def key_slots(value):
        return list(
            value.astype(LOW)
            .reshape(micros, kv_heads, n, p, part, head)
            .transpose(2, 3, 0, 4, 1, 5)
            .reshape(n, tokens, kv_width)
        )

    key_grad = scatter_slots(key_slots(key_piece), "seq", back_a)
    value_grad_low = scatter_slots(key_slots(value_piece), "seq", back_b).astype(LOW)
    query_pre_grad, key_pre_grad, grad_qgain, grad_kgain = heads_pull(
        (
            query_grad.reshape(tokens, q_heads, head) * scale,
            key_grad.reshape(tokens, kv_heads, head) * scale,
        )
    )
    query_pre_low = query_pre_grad.astype(LOW)
    kv_pre_low = jnp.concatenate([key_pre_grad.astype(LOW), value_grad_low], axis=1)

    def weight_grad(left, right, order):
        grad = dot_tn(left, right).astype(LOW)
        return scatter_slots(list(grad.reshape(n, block, right.shape[1])), "seq", order)

    grad_gating = weight_grad(normed, gate_pre_grad, back_a)
    grad_outproj = weight_grad(branch_grad, gated_low, back_b).T
    grad_query = weight_grad(normed, query_pre_low, back_a)
    grad_kv = weight_grad(normed, kv_pre_low, back_b)
    total = dot_nt(query_pre_low, w_q) + dot_nt(kv_pre_low, w_kv) + dot_nt(gate_pre_grad, w_g)
    normed_grad = permute_columns(collect_tp(total))
    norm_one_pull = jax.vjp(root_mean_square_scale, x_part, first_gain)[1]
    input_from, grad_first = norm_one_pull(normed_grad)
    input_grad = middle_grad + input_from

    gains = jnp.concatenate([grad_first, grad_second, grad_qgain, grad_kgain]).reshape(-1, head)
    gains = tree_sum(spread_tp(gains))
    for mask in masks:
        gains = gains + swap(gains, "seq", mask)
    gains = gains.reshape(-1)
    return (
        layer_rows.reshape(micros, part, width),
        input_grad.reshape(micros, part, width),
        gains[:width],
        grad_query,
        grad_kv[:, :kv_width],
        grad_kv[:, kv_width:],
        grad_gating,
        grad_outproj,
        gains[2 * width : 2 * width + head],
        gains[2 * width + head :],
        gains[width : 2 * width],
        grad_hgate,
        grad_hup,
        grad_hdown,
    )


def solution(mesh):
    in_specs = (
        P(None, "seq", None),
        P(None, "seq"),
        P(),
        P("seq", "tp"),
        P("seq", "tp"),
        P("seq", "tp"),
        P("seq", "tp"),
        P("tp", "seq"),
        P(),
        P(),
        P(),
        P("tp", "seq"),
        P("tp", "seq"),
        P("seq", "tp"),
        P(None, ("seq", "tp"), None),
    )
    out_specs = (
        P(None, ("seq", "tp"), None),
        P(None, ("seq", "tp"), None),
        P(),
        P("seq", "tp"),
        P("seq", "tp"),
        P("seq", "tp"),
        P("seq", "tp"),
        P("tp", "seq"),
        P(),
        P(),
        P(),
        P("tp", "seq"),
        P("tp", "seq"),
        P("seq", "tp"),
    )
    return jax.shard_map(
        per_device, mesh=mesh, in_specs=in_specs, out_specs=out_specs, check_vma=False
    )
```

```python
import jax
import jax.numpy as jnp
from jax import lax
from jax.experimental import pallas as pl
from jax.experimental.pallas import tpu as pltpu
from jax.sharding import PartitionSpec as P

EPS = 1e-06
ROPE_BASE = 5000000.0
NEG_LARGE = -1e30
F32 = jnp.float32
LOW = jnp.bfloat16
VMEM_LIMIT = 60 * 1024 * 1024


def shape_of(shape, dtype):
    return jax.ShapeDtypeStruct(shape, dtype)


def run_kernel(body, outs, args, flops, scalars=None):
    moved = sum(a.size * a.dtype.itemsize for a in args)
    moved += sum(o.size * o.dtype.itemsize for o in outs)
    specs = [pl.BlockSpec(memory_space=pltpu.VMEM)] * len(args)
    if scalars is not None:
        specs = [pl.BlockSpec(memory_space=pltpu.SMEM)] + specs
        args = [scalars] + list(args)
    return pl.pallas_call(
        body,
        out_shape=outs,
        in_specs=specs,
        out_specs=[pl.BlockSpec(memory_space=pltpu.VMEM)] * len(outs),
        compiler_params=pltpu.CompilerParams(vmem_limit_bytes=VMEM_LIMIT),
        cost_estimate=pl.CostEstimate(flops=flops, transcendentals=0, bytes_accessed=moved),
    )(*args)


def dot_nn(left, right):
    return jnp.dot(left, right, preferred_element_type=F32)


def dot_nt(left, right):
    return lax.dot_general(left, right, (((1,), (1,)), ((), ())), preferred_element_type=F32)


def dot_tn(left, right):
    return lax.dot_general(left, right, (((0,), (0,)), ((), ())), preferred_element_type=F32)


def rows_of(refs, place):
    return jnp.concatenate([refs[i][e] for i, e in (place[s] for s in range(len(place)))], axis=0)


def swap(value, axis, mask):
    count = lax.axis_size(axis)
    return lax.ppermute(value, axis, [(i, i ^ mask) for i in range(count)])


def gather_pieces(value, axis, order):
    pieces, place, slots = [value[None]], {0: (0, 0)}, [0]
    for mask in order[:-1]:
        sent = pieces[0] if len(pieces) == 1 else jnp.concatenate(pieces)
        last = slots
        pieces.append(swap(sent, axis, mask))
        got = [s ^ mask for s in slots]
        place.update({s: (len(pieces) - 1, i) for i, s in enumerate(got)})
        slots = slots + got
    for piece, ids in ((sent, last), (pieces[-1], got)):
        pieces.append(swap(piece, axis, order[-1]))
        place.update({s ^ order[-1]: (len(pieces) - 1, i) for i, s in enumerate(ids)})
    return pieces, place


def lane_order(order):
    return sorted(range(0, 2 << len(order), 2), key=lambda s: [s & mask for mask in order])


def join_lanes(keep, send):
    return keep.astype(F32) + swap(send, "seq", 1).astype(F32)


def scatter_step(total, mask, hold=None):
    half = total.shape[0] // 2
    got = swap(total[half:].astype(LOW), "seq", mask)
    if hold is not None:
        got = after(got, hold)
    return total[:half] + got.astype(F32)


def scatter_lanes(total, order):
    for mask in order:
        total = scatter_step(total, mask)
    return total


def exchange_tp(blocks):
    return lax.all_to_all(blocks, "tp", 0, 0, tiled=True)


def spread_tp(value):
    count = lax.axis_size("tp")
    return exchange_tp(jnp.broadcast_to(value[None], (count,) + value.shape))


def after(value, *earlier):
    return lax.optimization_barrier((value, earlier))[0]


def tree_sum(terms):
    while len(terms) > 1:
        terms = [terms[i] + terms[i + 1] for i in range(0, len(terms), 2)]
    return terms[0]


def inverse_rms(value):
    return lax.rsqrt(jnp.mean(value * value, axis=-1, keepdims=True) + EPS)


def per_device(
    layer_in,
    positions,
    first_gain,
    query_proj,
    key_projection,
    value_projection,
    gate_proj,
    output_proj,
    query_gain,
    key_norm_gain,
    second_gain,
    hidden_gate,
    hidden_up,
    hidden_down,
    out_cotangent,
):
    micros, local_rows, width = layer_in.shape
    head = query_gain.shape[0]
    n = lax.axis_size("seq")
    p = lax.axis_size("tp")
    me_seq = lax.axis_index("seq")
    me_tp = lax.axis_index("tp")
    me = jnp.stack([me_seq, me_tp]).astype(jnp.int32)
    part = local_rows // p
    tokens = micros * local_rows
    ptok = micros * part
    block = width // n
    chunk = width // p
    q_width = query_proj.shape[1]
    kv_width = key_projection.shape[1]
    q_heads = q_width // head
    kv_heads = kv_width // head
    group = q_heads // kv_heads
    units = hidden_down.shape[0] // p
    half_a = units // 2 // 16 * 16
    half_b = units - half_a
    total_rows = local_rows * n
    scale = head ** (-0.5)
    masks = [1 << b for b in range((n - 1).bit_length())]
    go_a = masks[1:] + masks[:1]
    go_b = masks[:0:-1] + masks[:1]
    back_a = masks[1:]
    back_b = masks[:0:-1]
    even = list(range(0, n, 2))
    odd = list(range(1, n, 2))
    lane_a, lane_b = lane_order(back_a), lane_order(back_b)
    inner = block % 128 == 0

    def permute_columns(value):
        return jnp.concatenate(
            [
                lax.dynamic_slice_in_dim(value, (me_seq ^ j) * block, block, value.ndim - 1)
                for j in range(n)
            ],
            axis=-1,
        )

    def outer_permute(value):
        return value if inner else permute_columns(value)

    def read_permuted(ref, me_ref):
        if not inner:
            return ref[...]
        where = [pl.multiple_of((me_ref[0] ^ j) * block, block) for j in range(n)]
        return jnp.concatenate([ref[:, pl.ds(w, block)] for w in where], axis=1)

    def write_blocks(value, ref):
        for b in range(p):
            for m in range(micros):
                start = m * local_rows + b * part
                ref[b, m * part : (m + 1) * part, :] = value[start : start + part].astype(LOW)

    def read_blocks(ref):
        return jnp.concatenate(
            [ref[b, m * part : (m + 1) * part, :] for m in range(micros) for b in range(p)], axis=0
        )

    def sum_blocks(ref):
        return tree_sum([ref[b].astype(F32) for b in range(p)])

    block_out = shape_of((p, ptok, width), LOW)

    w3 = jnp.stack([hidden_gate.T, hidden_up.T, hidden_down]).reshape(3, p, units, chunk)
    w3 = w3.transpose(1, 0, 2, 3)
    wire = exchange_tp(w3)

    w_q, q_place = gather_pieces(query_proj, "seq", go_a)
    w_kv, kv_place = gather_pieces(
        jnp.concatenate([key_projection, value_projection], axis=1), "seq", go_b
    )
    w_g, g_place = gather_pieces(gate_proj, "seq", go_a)
    w_o, o_place = gather_pieces(output_proj.T, "seq", go_b)
    steps = len(w_q)
    cot_part = out_cotangent.reshape(ptok, width)
    cot = spread_tp(after(cot_part, wire)).reshape(tokens, width)

    x_part = lax.dynamic_slice_in_dim(layer_in, me_tp * part, part, 1)
    x_part = x_part.reshape(ptok, width).astype(F32)
    x_rows = outer_permute(layer_in.reshape(tokens, width))
    places = positions.reshape(tokens)
    gain_row = outer_permute(first_gain[None])
    middle_lane = head // 2
    inverse = jnp.exp(-(jnp.arange(middle_lane, dtype=F32) * 2.0 / head) * jnp.log(ROPE_BASE))
    angles = places.astype(F32)[:, None] * inverse[None, :]
    cosine = jnp.concatenate([jnp.cos(angles), jnp.cos(angles)], axis=-1)
    sine = jnp.concatenate([-jnp.sin(angles), jnp.sin(angles)], axis=-1)
    q_gain = query_gain[None]
    k_gain = key_norm_gain[None]

    def split_refs(refs, *counts):
        out = []
        for c in counts:
            out.append(refs[:c])
            refs = refs[c:]
        return out + [refs]

    def heads_forward(pre, gain, cos, sin):
        out = []
        for h in range(pre.shape[1] // head):
            u = pre[:, h * head : (h + 1) * head]
            y = u * inverse_rms(u) * gain
            out.append(y * cos + pltpu.roll(y, middle_lane, 1) * sin)
        return jnp.concatenate(out, axis=1)

    def heads_backward(grad, pre, gain, cos, sin):
        out = []
        gain_grad = jnp.zeros((1, head), F32)
        for h in range(pre.shape[1] // head):
            u = pre[:, h * head : (h + 1) * head]
            g = grad[:, h * head : (h + 1) * head]
            r = inverse_rms(u)
            unit = u * r
            y = g * cos + pltpu.roll(g * sin, middle_lane, 1)
            gain_grad = gain_grad + jnp.sum(y * unit, axis=0, keepdims=True)
            t = y * gain
            out.append(r * (t - unit * jnp.mean(t * unit, axis=-1, keepdims=True)))
        return jnp.concatenate(out, axis=1), gain_grad

    def qkv_body(me_ref, x, gain, cos, sin, qg, kg, *refs):
        wq, wkv, outs = split_refs(refs, steps, steps)
        normed_out, qpre_out, kpre_out, q_out, k_out, v_out = outs
        rows = read_permuted(x, me_ref).astype(F32)
        low = (rows * inverse_rms(rows) * read_permuted(gain, me_ref)).astype(LOW)
        normed_out[...] = low
        kv = dot_nn(low, rows_of(wkv, kv_place))
        key = kv[:, :kv_width]
        kpre_out[...] = key
        v_out[...] = kv[:, kv_width:].astype(LOW)
        k_out[...] = heads_forward(key, kg[...], cos[...], sin[...]).astype(LOW)
        query = dot_nn(low, rows_of(wq, q_place))
        qpre_out[...] = query
        q_out[...] = heads_forward(query, qg[...], cos[...], sin[...]).astype(LOW)

    normed, query_pre, key_pre, query_low, key_low, value_low = run_kernel(
        qkv_body,
        [
            shape_of((tokens, width), LOW),
            shape_of((tokens, q_width), F32),
            shape_of((tokens, kv_width), F32),
            shape_of((tokens, q_width), LOW),
            shape_of((tokens, kv_width), LOW),
            shape_of((tokens, kv_width), LOW),
        ],
        [after(x_rows, w_g[1], w_o[1]), gain_row, cosine, sine, q_gain, k_gain, *w_q, *w_kv],
        2 * tokens * width * (q_width + 2 * kv_width),
        me,
    )
    keys, key_place = gather_pieces(key_low, "seq", go_a)
    values, value_place = gather_pieces(value_low, "seq", go_b)

    f_own = wire.transpose(1, 2, 0, 3).reshape(3, units, width)
    f_own = after(f_own, keys[-1], values[-1], w_g[-1], w_o[-1])
    f_a, fa_place = gather_pieces(f_own[:, :half_a], "seq", go_a)
    f_b, fb_place = gather_pieces(f_own[:, half_a:], "seq", go_b)

    inside = jnp.arange(local_rows, dtype=jnp.int32)
    query_pos = jnp.tile(me_seq * local_rows + inside, group)[:, None]
    key_pos = jnp.concatenate([(me_seq ^ j) * local_rows + inside for j in range(n)])[None, :]

    def group_rows(value, m, g):
        rows = value[m * local_rows : (m + 1) * local_rows]
        heads = range(g * group, (g + 1) * group)
        return jnp.concatenate([rows[:, h * head : (h + 1) * head] for h in heads], axis=0)

    def slot_rows(refs, place, m, g):
        rows = []
        for j in range(n):
            index, entry = place[j]
            start = m * local_rows
            at = (entry, slice(start, start + local_rows), slice(g * head, (g + 1) * head))
            rows.append(refs[index][at])
        return jnp.concatenate(rows, axis=0)

    def softmax_of(query, key, qpos, kpos):
        scores = jnp.where(kpos <= qpos, dot_nt(query, key) * scale, NEG_LARGE)
        weights = jnp.exp(scores - jnp.max(scores, axis=-1, keepdims=True))
        return weights * (1.0 / jnp.sum(weights, axis=-1, keepdims=True))

    def ungroup(pieces):
        rows = []
        for m in range(micros):
            columns = []
            for g in range(kv_heads):
                value = pieces[m, g]
                columns += [
                    value[h * local_rows : (h + 1) * local_rows] for h in range(group)
                ]
            rows.append(jnp.concatenate(columns, axis=1))
        return jnp.concatenate(rows, axis=0)

    def attend_body(q, normed_ref, qpos, kpos, *refs):
        ks, vs, wg, wo, outs = split_refs(refs, steps, steps, steps, steps)
        gate_out, att_out, gated_out, send_out = outs
        gate = dot_nn(normed_ref[...], rows_of(wg, g_place))
        gate_out[...] = gate
        query = q[...]
        pieces = {}
        for m in range(micros):
            for g in range(kv_heads):
                prob = softmax_of(
                    group_rows(query, m, g), slot_rows(ks, key_place, m, g), qpos[...], kpos[...]
                )
                pieces[m, g] = dot_nn(prob.astype(LOW), slot_rows(vs, value_place, m, g))
        att = ungroup(pieces)
        att_out[...] = att
        gated = (att * jax.nn.sigmoid(gate)).astype(LOW)
        gated_out[...] = gated
        write_blocks(dot_nt(gated, rows_of(wo, o_place)), send_out)

    att_flops = 4 * tokens * total_rows * q_width
    gate_pre, attended, gated_low, send = run_kernel(
        attend_body,
        [
            shape_of((tokens, q_width), F32),
            shape_of((tokens, q_width), F32),
            shape_of((tokens, q_width), LOW),
            block_out,
        ],
        [after(query_low, wire), normed, query_pos, key_pos, *keys, *values, *w_g, *w_o],
        att_flops + 4 * tokens * width * q_width,
    )
    got = exchange_tp(after(send, cot))

    def middle_body(me_ref, x, gain, got_ref, middle_out, low_out, total_ref):
        total_ref[...] = sum_blocks(got_ref)
        rows = x[...] + read_permuted(total_ref, me_ref)
        middle_out[...] = rows
        low = (rows * inverse_rms(rows) * gain[...]).astype(LOW)
        for b in range(p):
            low_out[b] = low

    def run_part(body, outs, args):
        specs = [pl.BlockSpec(memory_space=pltpu.SMEM)]
        specs += [pl.BlockSpec(memory_space=pltpu.VMEM)] * len(args)
        return pl.pallas_call(
            body,
            out_shape=outs,
            in_specs=specs,
            out_specs=[pl.BlockSpec(memory_space=pltpu.VMEM)] * len(outs),
            scratch_shapes=[pltpu.VMEM((ptok, width), F32)],
            compiler_params=pltpu.CompilerParams(vmem_limit_bytes=VMEM_LIMIT),
            cost_estimate=pl.CostEstimate(
                flops=20 * ptok * width, transcendentals=0, bytes_accessed=20 * ptok * width
            ),
        )(me, *args)

    part_f32 = shape_of((ptok, width), F32)
    gain_f32 = shape_of((1, width), F32)
    second = second_gain[None]
    middle, normed_two = run_part(
        middle_body,
        [part_f32, block_out],
        [x_part, second, outer_permute(got)],
    )
    n2 = exchange_tp(normed_two).reshape(tokens, width)

    lanes = n // 2
    halves = (half_a, half_b)
    lane_units = lanes * units
    pair = 2 if lanes % 2 == 0 else 1
    anywhere = pl.BlockSpec(memory_space=pl.ANY)
    whole = pl.BlockSpec(memory_space=pltpu.VMEM)
    f_places = (fa_place, fb_place)

    def start_loads(slots, refs, skipped, w, sem):
        count = len(refs) // 2
        loads = []
        for s, slot in enumerate(slots):
            for t in range(2):
                index, entry = f_places[t][slot]
                where = pl.ds(s * units + t * half_a, halves[t])
                source = refs[t * count + index - skipped].at[entry]
                copy = pltpu.make_async_copy(source, w.at[:, where, :], sem.at[2 * s + t])
                copy.start()
                loads.append(copy)
        return loads

    def pair_rows(step, loads):
        for copy in loads[2 * pair * step : 2 * pair * (step + 1)]:
            copy.wait()
        return slice(step * pair * units, (step + 1) * pair * units)

    def forward_body(x, *refs):
        held, outs, (w, sem) = split_refs(refs, 2 * steps, 7)
        out = None
        loads = start_loads(even + odd, held, 0, w, sem)
        for step in range(n // pair):
            rows = pair_rows(step, loads)
            lane = outs[: 3] if step < lanes // pair else outs[3:6]
            first_row = rows.start % lane_units
            at = slice(first_row, first_row + pair * units)
            gate = dot_nt(w[0, rows], x[...])
            up = dot_nt(w[1, rows], x[...])
            hidden = (gate * jax.nn.sigmoid(gate) * up).astype(LOW)
            lane[0][at] = gate
            lane[1][at] = up
            lane[2][at] = hidden
        out = dot_tn(outs[2][...], w[2, :lane_units]) + dot_tn(outs[5][...], w[2, lane_units:])
        outs[6][...] = out.astype(LOW)

    lane_outs = [
        shape_of((lane_units, tokens), F32),
        shape_of((lane_units, tokens), F32),
        shape_of((lane_units, tokens), LOW),
    ]
    *lane_acts, out_sum = pl.pallas_call(
        forward_body,
        out_shape=lane_outs + lane_outs + [shape_of((tokens, width), LOW)],
        in_specs=[whole] + [anywhere] * (2 * steps),
        out_specs=[whole] * 7,
        scratch_shapes=[
            pltpu.VMEM((3, 2 * lane_units, width), LOW),
            pltpu.SemaphoreType.DMA((2 * n,)),
        ],
        compiler_params=pltpu.CompilerParams(vmem_limit_bytes=VMEM_LIMIT),
        cost_estimate=pl.CostEstimate(
            flops=12 * tokens * width * lane_units,
            transcendentals=0,
            bytes_accessed=12 * lane_units * width + 8 * tokens * width,
        ),
    )(n2, *f_a, *f_b)
    acts_even, acts_odd = lane_acts[:3], lane_acts[3:]
    out_got = exchange_tp(out_sum.reshape(p, ptok, width))

    def backward_body(first, slots, count, x, c, gate_ref, up_ref, hid_ref, *refs):
        held, before, grads, (acc,), scratch = split_refs(
            refs, 2 * count, 0 if first else 1, 6, 1
        )
        w, low = scratch[:2]
        gbufs, in_sem, out_sem = scratch[2:8], scratch[8], scratch[9]
        loads = start_loads(slots, held, steps - 2 if first else 0, w, in_sem)
        stores = []

        def store(k, step, value):
            t, h = k % 2, halves[k % 2]
            for q in range(pair):
                slot = slots[step * pair + q] & ~1
                start = (lane_a, lane_b)[t].index(slot) * h
                at = pl.ds(start, h)
                source = q * units + t * half_a
                gbufs[k][start : start + h] = value[source : source + h]
                copy = pltpu.make_async_copy(
                    gbufs[k].at[at], grads[k].at[at], out_sem.at[6 * (step * pair + q) + k]
                )
                copy.start()
                stores.append(copy)

        for step in range(lanes // pair):
            rows = pair_rows(step, loads)
            gate, up = gate_ref[rows], up_ref[rows]
            grad = dot_nt(w[2, rows], c[...])
            sig = jax.nn.sigmoid(gate)
            gate_grad = (grad * up * sig * (1.0 + gate * (1.0 - sig))).astype(LOW)
            up_grad = (grad * gate * sig).astype(LOW)
            low[0, rows] = gate_grad
            low[1, rows] = up_grad
            sides = ((hid_ref[rows], c), (gate_grad, x), (up_grad, x))
            for i, (left, right) in zip((2, 0, 1), sides):
                value = dot_nn(left, right[...]).astype(LOW)
                store(2 * i, step, value)
                store(2 * i + 1, step, value)
        back = dot_tn(low[0], w[0]) + dot_tn(low[1], w[1])
        if not first:
            back = back + before[0][...]
        acc[...] = back.astype(acc.dtype)
        for copy in stores:
            copy.wait()

    def run_backward(first, dtype, slots, acts, *before):
        grad_outs = [shape_of((lanes * h, width), LOW) for _ in range(3) for h in halves]
        use = slice(steps - 2, steps) if first else slice(0, steps - 2)
        held = [*f_a[use], *f_b[use]]
        return pl.pallas_call(
            lambda *r: backward_body(first, slots, len(held) // 2, *r),
            out_shape=grad_outs + [shape_of((tokens, width), dtype)],
            in_specs=[whole] * 5 + [anywhere] * len(held) + [whole] * len(before),
            out_specs=[anywhere] * 6 + [whole],
            scratch_shapes=[
                pltpu.VMEM((3, lane_units, width), LOW),
                pltpu.VMEM((2, lane_units, tokens), LOW),
                *[pltpu.VMEM((lanes * h, width), LOW) for _ in range(3) for h in halves],
                pltpu.SemaphoreType.DMA((2 * lanes,)),
                pltpu.SemaphoreType.DMA((6 * lanes,)),
            ],
            compiler_params=pltpu.CompilerParams(vmem_limit_bytes=VMEM_LIMIT),
            cost_estimate=pl.CostEstimate(
                flops=12 * tokens * width * lane_units,
                transcendentals=0,
                bytes_accessed=12 * lane_units * width + 8 * tokens * width,
            ),
        )(n2, cot, *acts, *held, *before)

    *f_odd, back_odd = run_backward(True, F32, odd, acts_odd)
    *f_even, back_sum = run_backward(False, LOW, even, acts_even, back_odd)
    back_got = exchange_tp(back_sum.reshape(p, ptok, width))
    orders = (back_a, back_b)

    def first_steps(index):
        return [join_lanes(f_even[2 * index + t], f_odd[2 * index + t]) for t in range(2)]

    def next_steps(states, level, hold=None):
        return [scatter_step(total, orders[t][level], hold) for t, total in enumerate(states)]

    def last_steps(states, level, hold=None):
        for k in range(level, len(back_a)):
            states = next_steps(states, k, hold)
        return states

    def return_units(states, hold):
        blocks = jnp.concatenate(states).astype(LOW)
        blocks = blocks.reshape(units, p, chunk).transpose(1, 0, 2)
        return exchange_tp(after(blocks, hold)).reshape(p * units, chunk).astype(F32)

    down, gates, ups = first_steps(2), first_steps(0), first_steps(1)
    down = next_steps(down, 0)
    gates = next_steps(gates, 0)
    ups = [after(u, *down) for u in ups]
    down_last = last_steps(down, 1)
    gates_last = last_steps(gates, 1)

    def branch_body(me_ref, mid, cot_ref, gain, got_ref, mg_out, low_out, gain_out, scratch):
        total = sum_blocks(got_ref)
        rows = mid[...]
        r = inverse_rms(rows)
        unit = rows * r
        gain_out[...] = jnp.sum(total * unit, axis=0, keepdims=True)
        u = total * gain[...]
        grad = cot_ref[...].astype(F32) + r * (u - unit * jnp.mean(u * unit, -1, keepdims=True))
        mg_out[...] = grad
        scratch[...] = grad
        low = read_permuted(scratch, me_ref).astype(LOW)
        for b in range(p):
            low_out[b] = low

    middle_grad, branch_low, grad_second = run_part(
        branch_body,
        [part_f32, block_out, gain_f32],
        [after(middle, *ups), cot_part, second, back_got],
    )
    branch_grad = exchange_tp(outer_permute(branch_low))
    grad_hdown = return_units(down_last, branch_grad)

    def back_body(q, qpre, gate, att, cos, sin, qg, qpos, kpos, *refs):
        ks, vs, wo, (bg,), outs = split_refs(refs, steps, steps, steps, 1)
        k_odd, k_even, v_odd, v_even, dq_out, dg_out, bg_out, gain_out = outs
        branch = read_blocks(bg)
        bg_out[...] = branch
        gated_grad = dot_nn(branch, rows_of(wo, o_place))
        sig = jax.nn.sigmoid(gate[...])
        att_grad = (gated_grad * sig).astype(LOW)
        dg_out[...] = (gated_grad * att[...] * sig * (1.0 - sig)).astype(LOW)
        product = att_grad.astype(F32) * att[...]
        query = q[...]
        pieces = {}
        for m in range(micros):
            for g in range(kv_heads):
                qr = group_rows(query, m, g)
                ag = group_rows(att_grad, m, g)
                key = slot_rows(ks, key_place, m, g)
                value = slot_rows(vs, value_place, m, g)
                delta = jnp.sum(group_rows(product, m, g), axis=-1, keepdims=True)
                prob = softmax_of(qr, key, qpos[...], kpos[...])
                ds = (prob * (dot_nt(ag, value) - delta)).astype(LOW)
                pieces[m, g] = dot_nn(ds, key) * scale
                dk = dot_tn(ds, qr).astype(LOW)
                dv = dot_tn(prob.astype(LOW), ag).astype(LOW)
                for j in range(n):
                    src = slice(j * local_rows, (j + 1) * local_rows)
                    pairs = ((k_odd, k_even, lane_a, dk), (v_odd, v_even, lane_b, dv))
                    for odd_ref, even_ref, lane, value_grad in pairs:
                        dst = lane.index(j & ~1) * tokens + m * local_rows
                        at = (slice(dst, dst + local_rows), slice(g * head, (g + 1) * head))
                        (odd_ref if j % 2 else even_ref)[at] = value_grad[src]
        dq, gain_grad = heads_backward(ungroup(pieces), qpre[...], qg[...], cos[...], sin[...])
        dq_out[...] = dq.astype(LOW)
        gain_out[...] = gain_grad

    lane_kv = shape_of((lanes * tokens, kv_width), LOW)
    k_odd, k_even, v_odd, v_even, dq_low, dg_low, branch_rows, grad_qgain = run_kernel(
        back_body,
        [
            lane_kv,
            lane_kv,
            lane_kv,
            lane_kv,
            shape_of((tokens, q_width), LOW),
            shape_of((tokens, q_width), LOW),
            shape_of((tokens, width), LOW),
            shape_of((1, head), F32),
        ],
        [
            after(query_low, *down_last, *gates),
            query_pre,
            gate_pre,
            attended,
            cosine,
            sine,
            q_gain,
            query_pos,
            key_pos,
            *keys,
            *values,
            *w_o,
            branch_grad,
        ],
        5 * att_flops // 2 + 2 * tokens * width * q_width,
    )
    key_grad = scatter_lanes(join_lanes(k_even, k_odd), back_a)
    value_grad = scatter_lanes(join_lanes(v_even, v_odd), back_b)

    def write_lanes(value, odd_ref, even_ref, lane):
        for j in range(n):
            place = lane.index(j & ~1)
            at = slice(place * block, (place + 1) * block)
            (odd_ref if j % 2 else even_ref)[at] = value[j * block : (j + 1) * block].astype(LOW)

    lane_w = shape_of((lanes * block, q_width), LOW)

    def weight_body(normed_ref, dq, dg, bg, gated, *refs):
        wq, wg, outs = split_refs(refs, steps, steps)
        g_odd, g_even, o_odd, o_even, q_odd, q_even, acc = outs
        low = normed_ref[...]
        write_lanes(dot_tn(low, dg[...]), g_odd, g_even, lane_a)
        write_lanes(dot_tn(bg[...], gated[...]), o_odd, o_even, lane_b)
        write_lanes(dot_tn(low, dq[...]), q_odd, q_even, lane_a)
        acc[...] = dot_nt(dq[...], rows_of(wq, q_place)) + dot_nt(dg[...], rows_of(wg, g_place))

    g_odd, g_even, o_odd, o_even, q_odd, q_even, normed_acc = run_kernel(
        weight_body,
        [lane_w] * 6 + [shape_of((tokens, width), F32)],
        [normed, dq_low, dg_low, branch_rows, gated_low, *w_q, *w_g],
        10 * tokens * width * q_width,
    )

    def key_body(dk, dv, kpre, cos, sin, kg, normed_ref, acc, *refs):
        wkv, (kv_odd, kv_even, gain_out, send_out) = split_refs(refs, steps)
        dkey, gain_grad = heads_backward(
            dk[...] * scale, kpre[...], kg[...], cos[...], sin[...]
        )
        gain_out[...] = gain_grad
        low = jnp.concatenate([dkey.astype(LOW), dv[...].astype(LOW)], axis=1)
        write_blocks(acc[...] + dot_nt(low, rows_of(wkv, kv_place)), send_out)
        write_lanes(dot_tn(normed_ref[...], low), kv_odd, kv_even, lane_b)

    lane_w2 = shape_of((lanes * block, 2 * kv_width), LOW)
    kv_odd, kv_even, grad_kgain, send = run_kernel(
        key_body,
        [lane_w2, lane_w2, shape_of((1, head), F32), block_out],
        [key_grad, value_grad, key_pre, cosine, sine, k_gain, normed, normed_acc, *w_kv],
        8 * tokens * width * kv_width,
    )
    gate_raw = return_units(gates_last, grad_hdown)
    got = exchange_tp(after(send, gate_raw))
    ups = last_steps(next_steps(ups, 0, normed_acc), 1)
    up_raw = return_units(ups, got)
    ready = (key_grad, value_grad)
    g_odd, o_odd, q_odd = after((g_odd, o_odd, q_odd), *ready)
    grad_gating = scatter_lanes(join_lanes(g_even, g_odd), back_a)
    grad_outproj = scatter_lanes(join_lanes(o_even, o_odd), back_b).T
    grad_query = scatter_lanes(join_lanes(q_even, q_odd), back_a)
    grad_kv = scatter_lanes(join_lanes(kv_even, kv_odd), back_b)

    def input_body(me_ref, x, gain, mg, got_ref, in_out, gain_out, total_ref):
        total_ref[...] = sum_blocks(got_ref)
        total = read_permuted(total_ref, me_ref)
        rows = x[...]
        r = inverse_rms(rows)
        unit = rows * r
        gain_out[...] = jnp.sum(total * unit, axis=0, keepdims=True)
        u = total * gain[...]
        in_out[...] = mg[...] + r * (u - unit * jnp.mean(u * unit, -1, keepdims=True))

    input_grad, grad_first = run_part(
        input_body,
        [part_f32, gain_f32],
        [x_part, first_gain[None], middle_grad, outer_permute(got)],
    )
    gains = jnp.concatenate([grad_first, grad_second, grad_qgain, grad_kgain], axis=1)
    gains = gains.reshape(-1, head)
    gains = tree_sum(list(spread_tp(gains)))
    for mask in masks:
        gains = gains + swap(gains, "seq", mask)
    gains = gains.reshape(-1)

    ffn_out = tree_sum([out_got[b].astype(F32) for b in range(p)])
    layer_rows = (middle + ffn_out).astype(LOW)

    grad_hgate = gate_raw.T
    grad_hup = up_raw.T
    return (
        layer_rows.reshape(micros, part, width),
        input_grad.reshape(micros, part, width),
        gains[:width],
        grad_query,
        grad_kv[:, :kv_width],
        grad_kv[:, kv_width:],
        grad_gating,
        grad_outproj,
        gains[2 * width : 2 * width + head],
        gains[2 * width + head :],
        gains[width : 2 * width],
        grad_hgate,
        grad_hup,
        grad_hdown,
    )


def solution(mesh):
    in_specs = (
        P(None, "seq", None),
        P(None, "seq"),
        P(),
        P("seq", "tp"),
        P("seq", "tp"),
        P("seq", "tp"),
        P("seq", "tp"),
        P("tp", "seq"),
        P(),
        P(),
        P(),
        P("tp", "seq"),
        P("tp", "seq"),
        P("seq", "tp"),
        P(None, ("seq", "tp"), None),
    )
    out_specs = (
        P(None, ("seq", "tp"), None),
        P(None, ("seq", "tp"), None),
        P(),
        P("seq", "tp"),
        P("seq", "tp"),
        P("seq", "tp"),
        P("seq", "tp"),
        P("tp", "seq"),
        P(),
        P(),
        P(),
        P("tp", "seq"),
        P("tp", "seq"),
        P("seq", "tp"),
    )
    return jax.shard_map(
        per_device, mesh=mesh, in_specs=in_specs, out_specs=out_specs, check_vma=False
    )
```

```python
import jax
import jax.numpy as jnp
from jax import lax
from jax.experimental import pallas as pl
from jax.experimental.pallas import tpu as pltpu
from jax.sharding import PartitionSpec as P

EPS = 1e-06
ROPE_BASE = 5000000.0
NEG_LARGE = -1e30
F32 = jnp.float32
LOW = jnp.bfloat16
VMEM_LIMIT = 60 * 1024 * 1024


def shape_of(shape, dtype):
    return jax.ShapeDtypeStruct(shape, dtype)


def run_kernel(body, outs, args, flops, scalars=None):
    moved = sum(a.size * a.dtype.itemsize for a in args)
    moved += sum(o.size * o.dtype.itemsize for o in outs)
    specs = [pl.BlockSpec(memory_space=pltpu.VMEM)] * len(args)
    if scalars is not None:
        specs = [pl.BlockSpec(memory_space=pltpu.SMEM)] + specs
        args = [scalars] + list(args)
    return pl.pallas_call(
        body,
        out_shape=outs,
        in_specs=specs,
        out_specs=[pl.BlockSpec(memory_space=pltpu.VMEM)] * len(outs),
        compiler_params=pltpu.CompilerParams(vmem_limit_bytes=VMEM_LIMIT),
        cost_estimate=pl.CostEstimate(
            flops=flops // 8, transcendentals=0, bytes_accessed=moved // 8
        ),
    )(*args)


def dot_nn(left, right):
    return jnp.dot(left, right, preferred_element_type=F32)


def dot_nt(left, right):
    return lax.dot_general(left, right, (((1,), (1,)), ((), ())), preferred_element_type=F32)


def dot_tn(left, right):
    return lax.dot_general(left, right, (((0,), (0,)), ((), ())), preferred_element_type=F32)


def rows_of(refs, place):
    return jnp.concatenate([refs[i][e] for i, e in (place[s] for s in range(len(place)))], axis=0)


def swap(value, axis, mask):
    count = lax.axis_size(axis)
    return lax.ppermute(value, axis, [(i, i ^ mask) for i in range(count)])


def gather_pieces(value, axis, order, hold=None, hold_last=None):
    pieces, place, slots = [value[None]], {0: (0, 0)}, [0]
    for mask in order[:-1]:
        sent = pieces[0] if len(pieces) == 1 else jnp.concatenate(pieces)
        if hold is not None and len(pieces) == 2:
            sent = after(sent, hold)
        last = slots
        pieces.append(swap(sent, axis, mask))
        got = [s ^ mask for s in slots]
        place.update({s: (len(pieces) - 1, i) for i, s in enumerate(got)})
        slots = slots + got
    received = pieces[-1] if hold_last is None else after(pieces[-1], hold_last)
    for piece, ids in ((sent, last), (received, got)):
        pieces.append(swap(piece, axis, order[-1]))
        place.update({s ^ order[-1]: (len(pieces) - 1, i) for i, s in enumerate(ids)})
    return pieces, place


def lane_order(order):
    return sorted(range(0, 2 << len(order), 2), key=lambda s: [s & mask for mask in order])


def sum_halves(keep, got, last):
    if last:
        return keep.astype(F32) + got.astype(F32)
    half = keep.shape[0] // 2
    sides = (slice(None, half), slice(half, None))
    return tuple((keep[at].astype(F32) + got[at].astype(F32)).astype(LOW) for at in sides)


def join_lanes(keep, send, last=False):
    return sum_halves(keep, swap(send, "seq", 1), last)


def scatter_step(halves, mask, last, hold=None):
    keep, send = halves
    got = swap(send, "seq", mask)
    if hold is not None:
        got = after(got, hold)
    return sum_halves(keep, got, last)


def scatter_lanes(total, order):
    for mask in order:
        total = scatter_step(total, mask, mask == order[-1])
    return total


def exchange_tp(blocks):
    return lax.all_to_all(blocks, "tp", 0, 0, tiled=True)


def spread_tp(value):
    count = lax.axis_size("tp")
    return exchange_tp(jnp.broadcast_to(value[None], (count,) + value.shape))


def after(value, *earlier):
    return lax.optimization_barrier((value, earlier))[0]


def tree_sum(terms):
    while len(terms) > 1:
        terms = [terms[i] + terms[i + 1] for i in range(0, len(terms), 2)]
    return terms[0]


def inverse_rms(value):
    return lax.rsqrt(jnp.mean(value * value, axis=-1, keepdims=True) + EPS)


def per_device(
    layer_in,
    positions,
    first_gain,
    query_proj,
    key_projection,
    value_projection,
    gate_proj,
    output_proj,
    query_gain,
    key_norm_gain,
    second_gain,
    hidden_gate,
    hidden_up,
    hidden_down,
    out_cotangent,
):
    micros, local_rows, width = layer_in.shape
    head = query_gain.shape[0]
    n = lax.axis_size("seq")
    p = lax.axis_size("tp")
    me_seq = lax.axis_index("seq")
    me_tp = lax.axis_index("tp")
    me = jnp.stack([me_seq, me_tp]).astype(jnp.int32)
    part = local_rows // p
    tokens = micros * local_rows
    ptok = micros * part
    block = width // n
    chunk = width // p
    q_width = query_proj.shape[1]
    kv_width = key_projection.shape[1]
    q_heads = q_width // head
    kv_heads = kv_width // head
    group = q_heads // kv_heads
    units = hidden_down.shape[0] // p
    half_a = units // 2 // 16 * 16
    half_b = units - half_a
    total_rows = local_rows * n
    scale = head ** (-0.5)
    masks = [1 << b for b in range((n - 1).bit_length())]
    go_a = masks[1:] + masks[:1]
    go_b = masks[:0:-1] + masks[:1]
    back_a = masks[1:]
    back_b = masks[:0:-1]
    even = list(range(0, n, 2))
    odd = list(range(1, n, 2))
    lane_a, lane_b = lane_order(back_a), lane_order(back_b)
    inner = block % 128 == 0

    def permute_columns(value):
        return jnp.concatenate(
            [
                lax.dynamic_slice_in_dim(value, (me_seq ^ j) * block, block, value.ndim - 1)
                for j in range(n)
            ],
            axis=-1,
        )

    def outer_permute(value):
        return value if inner else permute_columns(value)

    def read_permuted(ref, me_ref):
        if not inner:
            return ref[...]
        where = [pl.multiple_of((me_ref[0] ^ j) * block, block) for j in range(n)]
        return jnp.concatenate([ref[:, pl.ds(w, block)] for w in where], axis=1)

    def write_blocks(value, ref):
        for b in range(p):
            for m in range(micros):
                start = m * local_rows + b * part
                ref[b, m * part : (m + 1) * part, :] = value[start : start + part].astype(LOW)

    def read_blocks(ref):
        return jnp.concatenate(
            [ref[b, m * part : (m + 1) * part, :] for m in range(micros) for b in range(p)], axis=0
        )

    def sum_blocks(ref):
        return tree_sum([ref[b].astype(F32) for b in range(p)])

    block_out = shape_of((p, ptok, width), LOW)

    w3 = jnp.stack([hidden_gate.T, hidden_up.T, hidden_down]).reshape(3, p, units, chunk)
    w3 = w3.transpose(1, 0, 2, 3)

    w_q, q_place = gather_pieces(query_proj, "seq", go_a)
    w_kv, kv_place = gather_pieces(
        jnp.concatenate([key_projection, value_projection], axis=1), "seq", go_b
    )
    w_g, g_place = gather_pieces(gate_proj, "seq", go_a)
    w_o, o_place = gather_pieces(output_proj.T, "seq", go_b)
    steps = len(w_q)
    wire = exchange_tp(after(w3, w_q[1], w_kv[1]))
    cot_part = out_cotangent.reshape(ptok, width)
    cot = spread_tp(after(cot_part, wire)).reshape(tokens, width)

    x_part = lax.dynamic_slice_in_dim(layer_in, me_tp * part, part, 1)
    x_part = x_part.reshape(ptok, width).astype(F32)
    x_rows = outer_permute(layer_in.reshape(tokens, width))
    places = positions.reshape(tokens)
    gain_row = outer_permute(first_gain[None])
    middle_lane = head // 2
    inverse = jnp.exp(-(jnp.arange(middle_lane, dtype=F32) * 2.0 / head) * jnp.log(ROPE_BASE))
    angles = places.astype(F32)[:, None] * inverse[None, :]
    cosine = jnp.concatenate([jnp.cos(angles), jnp.cos(angles)], axis=-1)
    sine = jnp.concatenate([-jnp.sin(angles), jnp.sin(angles)], axis=-1)
    q_gain = query_gain[None]
    k_gain = key_norm_gain[None]

    def split_refs(refs, *counts):
        out = []
        for c in counts:
            out.append(refs[:c])
            refs = refs[c:]
        return out + [refs]

    def heads_forward(pre, gain, cos, sin):
        out = []
        for h in range(pre.shape[1] // head):
            u = pre[:, h * head : (h + 1) * head]
            y = u * inverse_rms(u) * gain
            out.append(y * cos + pltpu.roll(y, middle_lane, 1) * sin)
        return jnp.concatenate(out, axis=1)

    def heads_backward(grad, pre, gain, cos, sin):
        out = []
        gain_grad = jnp.zeros((1, head), F32)
        for h in range(pre.shape[1] // head):
            u = pre[:, h * head : (h + 1) * head]
            g = grad[:, h * head : (h + 1) * head]
            r = inverse_rms(u)
            unit = u * r
            y = g * cos + pltpu.roll(g * sin, middle_lane, 1)
            gain_grad = gain_grad + jnp.sum(y * unit, axis=0, keepdims=True)
            t = y * gain
            out.append(r * (t - unit * jnp.mean(t * unit, axis=-1, keepdims=True)))
        return jnp.concatenate(out, axis=1), gain_grad

    def qkv_body(me_ref, x, gain, cos, sin, qg, kg, *refs):
        wq, wkv, outs = split_refs(refs, steps, steps)
        normed_out, qpre_out, kpre_out, q_out, k_out, v_out = outs
        rows = read_permuted(x, me_ref).astype(F32)
        low = (rows * inverse_rms(rows) * read_permuted(gain, me_ref)).astype(LOW)
        normed_out[...] = low
        kv = dot_nn(low, rows_of(wkv, kv_place))
        key = kv[:, :kv_width]
        kpre_out[...] = key
        v_out[...] = kv[:, kv_width:].astype(LOW)
        k_out[...] = heads_forward(key, kg[...], cos[...], sin[...]).astype(LOW)
        query = dot_nn(low, rows_of(wq, q_place))
        qpre_out[...] = query
        q_out[...] = heads_forward(query, qg[...], cos[...], sin[...]).astype(LOW)

    normed, query_pre, key_pre, query_low, key_low, value_low = run_kernel(
        qkv_body,
        [
            shape_of((tokens, width), LOW),
            shape_of((tokens, q_width), F32),
            shape_of((tokens, kv_width), F32),
            shape_of((tokens, q_width), LOW),
            shape_of((tokens, kv_width), LOW),
            shape_of((tokens, kv_width), LOW),
        ],
        [after(x_rows, w_g[1], w_o[1]), gain_row, cosine, sine, q_gain, k_gain, *w_q, *w_kv],
        2 * tokens * width * (q_width + 2 * kv_width),
        me,
    )
    keys, key_place = gather_pieces(key_low, "seq", go_a)
    values, value_place = gather_pieces(value_low, "seq", go_b)

    f_own = wire.transpose(1, 2, 0, 3).reshape(3, units, width)
    f_own = after(f_own, keys[-1], values[-1], w_g[-1], w_o[-1])

    inside = jnp.arange(local_rows, dtype=jnp.int32)
    query_pos = jnp.tile(me_seq * local_rows + inside, group)[:, None]
    key_pos = jnp.concatenate([(me_seq ^ j) * local_rows + inside for j in range(n)])[None, :]

    def group_rows(value, m, g):
        rows = value[m * local_rows : (m + 1) * local_rows]
        heads = range(g * group, (g + 1) * group)
        return jnp.concatenate([rows[:, h * head : (h + 1) * head] for h in heads], axis=0)

    def slot_rows(refs, place, m, g):
        rows = []
        for j in range(n):
            index, entry = place[j]
            start = m * local_rows
            at = (entry, slice(start, start + local_rows), slice(g * head, (g + 1) * head))
            rows.append(refs[index][at])
        return jnp.concatenate(rows, axis=0)

    def softmax_of(query, key, qpos, kpos):
        scores = jnp.where(kpos <= qpos, dot_nt(query, key) * scale, NEG_LARGE)
        weights = jnp.exp(scores - jnp.max(scores, axis=-1, keepdims=True))
        return weights * (1.0 / jnp.sum(weights, axis=-1, keepdims=True))

    def ungroup(pieces):
        rows = []
        for m in range(micros):
            columns = []
            for g in range(kv_heads):
                value = pieces[m, g]
                columns += [
                    value[h * local_rows : (h + 1) * local_rows] for h in range(group)
                ]
            rows.append(jnp.concatenate(columns, axis=1))
        return jnp.concatenate(rows, axis=0)

    def attend_body(q, normed_ref, qpos, kpos, *refs):
        ks, vs, wg, wo, outs = split_refs(refs, steps, steps, steps, steps)
        gate_out, att_out, gated_out, send_out = outs
        gate = dot_nn(normed_ref[...], rows_of(wg, g_place))
        gate_out[...] = gate
        query = q[...]
        pieces = {}
        for m in range(micros):
            for g in range(kv_heads):
                prob = softmax_of(
                    group_rows(query, m, g), slot_rows(ks, key_place, m, g), qpos[...], kpos[...]
                )
                pieces[m, g] = dot_nn(prob.astype(LOW), slot_rows(vs, value_place, m, g))
        att = ungroup(pieces)
        att_out[...] = att
        gated = (att * jax.nn.sigmoid(gate)).astype(LOW)
        gated_out[...] = gated
        write_blocks(dot_nt(gated, rows_of(wo, o_place)), send_out)

    att_flops = 4 * tokens * total_rows * q_width
    gate_pre, attended, gated_low, send = run_kernel(
        attend_body,
        [
            shape_of((tokens, q_width), F32),
            shape_of((tokens, q_width), F32),
            shape_of((tokens, q_width), LOW),
            block_out,
        ],
        [after(query_low, wire), normed, query_pos, key_pos, *keys, *values, *w_g, *w_o],
        att_flops + 4 * tokens * width * q_width,
    )
    got = exchange_tp(after(send, cot))

    def middle_body(me_ref, x, gain, got_ref, middle_out, low_out, total_ref):
        total_ref[...] = sum_blocks(got_ref)
        rows = x[...] + read_permuted(total_ref, me_ref)
        middle_out[...] = rows
        low = (rows * inverse_rms(rows) * gain[...]).astype(LOW)
        for b in range(p):
            low_out[b] = low

    def run_part(body, outs, args):
        specs = [pl.BlockSpec(memory_space=pltpu.SMEM)]
        specs += [pl.BlockSpec(memory_space=pltpu.VMEM)] * len(args)
        return pl.pallas_call(
            body,
            out_shape=outs,
            in_specs=specs,
            out_specs=[pl.BlockSpec(memory_space=pltpu.VMEM)] * len(outs),
            scratch_shapes=[pltpu.VMEM((ptok, width), F32)],
            compiler_params=pltpu.CompilerParams(vmem_limit_bytes=VMEM_LIMIT),
            cost_estimate=pl.CostEstimate(
                flops=20 * ptok * width, transcendentals=0, bytes_accessed=20 * ptok * width
            ),
        )(me, *args)

    part_f32 = shape_of((ptok, width), F32)
    gain_f32 = shape_of((1, width), F32)
    second = second_gain[None]
    middle, normed_two = run_part(
        middle_body,
        [part_f32, block_out],
        [x_part, second, outer_permute(got)],
    )
    n2 = exchange_tp(normed_two).reshape(tokens, width)
    f_a, fa_place = gather_pieces(f_own[:, :half_a], "seq", go_a, send, n2)
    f_b, fb_place = gather_pieces(f_own[:, half_a:], "seq", go_b, send, n2)

    lanes = n // 2
    halves = (half_a, half_b)
    lane_units = lanes * units
    pair = 2 if lanes % 2 == 0 else 1
    anywhere = pl.BlockSpec(memory_space=pl.ANY)
    whole = pl.BlockSpec(memory_space=pltpu.VMEM)
    f_places = (fa_place, fb_place)

    def start_loads(slots, refs, skipped, w, sem):
        count = len(refs) // 2
        loads = []
        for s, slot in enumerate(slots):
            for t in range(2):
                index, entry = f_places[t][slot]
                where = pl.ds(s * units + t * half_a, halves[t])
                source = refs[t * count + index - skipped].at[entry]
                copy = pltpu.make_async_copy(source, w.at[:, where, :], sem.at[2 * s + t])
                copy.start()
                loads.append(copy)
        return loads

    def pair_rows(step, loads):
        for copy in loads[2 * pair * step : 2 * pair * (step + 1)]:
            copy.wait()
        return slice(step * pair * units, (step + 1) * pair * units)

    def forward_body(last, slots, count, x, *refs):
        held, before, outs, (w, sem) = split_refs(refs, 2 * count, 1 if last else 0, 4)
        loads = start_loads(slots, held, steps - 2 if last else 0, w, sem)
        for step in range(lanes // pair):
            rows = pair_rows(step, loads)
            gate = dot_nt(w[0, rows], x[...])
            up = dot_nt(w[1, rows], x[...])
            outs[0][rows] = gate
            outs[1][rows] = up
            outs[2][rows] = (gate * jax.nn.sigmoid(gate) * up).astype(LOW)
        out = dot_tn(outs[2][...], w[2])
        if last:
            out = out + before[0][...]
        outs[3][...] = out.astype(outs[3].dtype)

    def run_forward(last, dtype, slots, *before):
        use = slice(steps - 2, steps) if last else slice(0, steps - 2)
        held = [*f_a[use], *f_b[use]]
        return pl.pallas_call(
            lambda *r: forward_body(last, slots, len(held) // 2, *r),
            out_shape=[
                shape_of((lane_units, tokens), F32),
                shape_of((lane_units, tokens), F32),
                shape_of((lane_units, tokens), LOW),
                shape_of((tokens, width), dtype),
            ],
            in_specs=[whole] + [anywhere] * len(held) + [whole] * len(before),
            out_specs=[whole] * 4,
            scratch_shapes=[
                pltpu.VMEM((3, lane_units, width), LOW),
                pltpu.SemaphoreType.DMA((2 * lanes,)),
            ],
            compiler_params=pltpu.CompilerParams(vmem_limit_bytes=VMEM_LIMIT),
            cost_estimate=pl.CostEstimate(
                flops=6 * tokens * width * lane_units // 8,
                transcendentals=0,
                bytes_accessed=(6 * lane_units * width + 4 * tokens * width) // 8,
            ),
        )(n2, *held, *before)

    *acts_even, out_even = run_forward(False, F32, even)
    *acts_odd, out_sum = run_forward(True, LOW, odd, out_even)
    out_got = exchange_tp(out_sum.reshape(p, ptok, width))

    def backward_body(first, slots, count, x, c, gate_ref, up_ref, hid_ref, *refs):
        held, before, grads, (acc,), scratch = split_refs(
            refs, 2 * count, 0 if first else 1, 6, 1
        )
        w, low = scratch[:2]
        gbufs, in_sem, out_sem = scratch[2:8], scratch[8], scratch[9]
        loads = start_loads(slots, held, steps - 2 if first else 0, w, in_sem)
        stores = []

        def store(k, step, value):
            t, h = k % 2, halves[k % 2]
            for q in range(pair):
                slot = slots[step * pair + q] & ~1
                start = (lane_a, lane_b)[t].index(slot) * h
                at = pl.ds(start, h)
                source = q * units + t * half_a
                gbufs[k][start : start + h] = value[source : source + h]
                copy = pltpu.make_async_copy(
                    gbufs[k].at[at], grads[k].at[at], out_sem.at[6 * (step * pair + q) + k]
                )
                copy.start()
                stores.append(copy)

        for step in range(lanes // pair):
            rows = pair_rows(step, loads)
            gate, up = gate_ref[rows], up_ref[rows]
            grad = dot_nt(w[2, rows], c[...])
            sig = jax.nn.sigmoid(gate)
            gate_grad = (grad * up * sig * (1.0 + gate * (1.0 - sig))).astype(LOW)
            up_grad = (grad * gate * sig).astype(LOW)
            low[0, rows] = gate_grad
            low[1, rows] = up_grad
            sides = ((hid_ref[rows], c), (gate_grad, x), (up_grad, x))
            for i, (left, right) in zip((2, 0, 1), sides):
                value = dot_nn(left, right[...]).astype(LOW)
                store(2 * i, step, value)
                store(2 * i + 1, step, value)
        back = dot_tn(low[0], w[0]) + dot_tn(low[1], w[1])
        if not first:
            back = back + before[0][...]
        acc[...] = back.astype(acc.dtype)
        for copy in stores:
            copy.wait()

    def run_backward(first, dtype, slots, acts, *before):
        grad_outs = [shape_of((lanes * h, width), LOW) for _ in range(3) for h in halves]
        use = slice(steps - 2, steps) if first else slice(0, steps - 2)
        held = [*f_a[use], *f_b[use]]
        return pl.pallas_call(
            lambda *r: backward_body(first, slots, len(held) // 2, *r),
            out_shape=grad_outs + [shape_of((tokens, width), dtype)],
            in_specs=[whole] * 5 + [anywhere] * len(held) + [whole] * len(before),
            out_specs=[anywhere] * 6 + [whole],
            scratch_shapes=[
                pltpu.VMEM((3, lane_units, width), LOW),
                pltpu.VMEM((2, lane_units, tokens), LOW),
                *[pltpu.VMEM((lanes * h, width), LOW) for _ in range(3) for h in halves],
                pltpu.SemaphoreType.DMA((2 * lanes,)),
                pltpu.SemaphoreType.DMA((6 * lanes,)),
            ],
            compiler_params=pltpu.CompilerParams(vmem_limit_bytes=VMEM_LIMIT),
            cost_estimate=pl.CostEstimate(
                flops=12 * tokens * width * lane_units // 8,
                transcendentals=0,
                bytes_accessed=(12 * lane_units * width + 8 * tokens * width) // 8,
            ),
        )(n2, cot, *acts, *held, *before)

    *f_odd, back_odd = run_backward(True, F32, odd, acts_odd)
    *f_even, back_sum = run_backward(False, LOW, even, acts_even, back_odd)
    back_got = exchange_tp(after(back_sum, out_got).reshape(p, ptok, width))
    orders = (back_a, back_b)

    def first_steps(index):
        return [join_lanes(f_even[2 * index + t], f_odd[2 * index + t]) for t in range(2)]

    def next_steps(states, level, hold=None):
        last = level == len(back_a) - 1
        return [
            scatter_step(state, orders[t][level], last, hold) for t, state in enumerate(states)
        ]

    def last_steps(states, level, hold=None):
        for k in range(level, len(back_a)):
            states = next_steps(states, k, hold)
        return states

    def return_units(states, hold):
        blocks = jnp.concatenate(states).astype(LOW)
        blocks = blocks.reshape(units, p, chunk).transpose(1, 0, 2)
        raw = exchange_tp(after(blocks, hold))
        return raw, raw.reshape(p * units, chunk).astype(F32)

    down, gates, ups = first_steps(2), first_steps(0), first_steps(1)
    down = next_steps(down, 0)

    def branch_body(me_ref, mid, cot_ref, gain, got_ref, mg_out, low_out, gain_out, scratch):
        total = sum_blocks(got_ref)
        rows = mid[...]
        r = inverse_rms(rows)
        unit = rows * r
        gain_out[...] = jnp.sum(total * unit, axis=0, keepdims=True)
        u = total * gain[...]
        grad = cot_ref[...].astype(F32) + r * (u - unit * jnp.mean(u * unit, -1, keepdims=True))
        mg_out[...] = grad
        scratch[...] = grad
        low = read_permuted(scratch, me_ref).astype(LOW)
        for b in range(p):
            low_out[b] = low

    middle_grad, branch_low, grad_second = run_part(
        branch_body,
        [part_f32, block_out, gain_f32],
        [middle, cot_part, second, back_got],
    )
    branch_grad = exchange_tp(outer_permute(branch_low))
    gates = next_steps(gates, 0, branch_low)
    ups = [after(u, *down) for u in ups]
    down_last = last_steps(down, 1, branch_low)
    down_raw, grad_hdown = return_units(down_last, branch_grad)

    def back_body(q, qpre, gate, att, cos, sin, qg, qpos, kpos, *refs):
        ks, vs, wo, (bg,), outs = split_refs(refs, steps, steps, steps, 1)
        k_odd, k_even, v_odd, v_even, dq_out, dg_out, bg_out, gain_out = outs
        branch = read_blocks(bg)
        bg_out[...] = branch
        gated_grad = dot_nn(branch, rows_of(wo, o_place))
        sig = jax.nn.sigmoid(gate[...])
        att_grad = (gated_grad * sig).astype(LOW)
        dg_out[...] = (gated_grad * att[...] * sig * (1.0 - sig)).astype(LOW)
        product = att_grad.astype(F32) * att[...]
        query = q[...]
        pieces = {}
        for m in range(micros):
            for g in range(kv_heads):
                qr = group_rows(query, m, g)
                ag = group_rows(att_grad, m, g)
                key = slot_rows(ks, key_place, m, g)
                value = slot_rows(vs, value_place, m, g)
                delta = jnp.sum(group_rows(product, m, g), axis=-1, keepdims=True)
                prob = softmax_of(qr, key, qpos[...], kpos[...])
                ds = (prob * (dot_nt(ag, value) - delta)).astype(LOW)
                pieces[m, g] = dot_nn(ds, key) * scale
                dk = dot_tn(ds, qr).astype(LOW)
                dv = dot_tn(prob.astype(LOW), ag).astype(LOW)
                for j in range(n):
                    src = slice(j * local_rows, (j + 1) * local_rows)
                    pairs = ((k_odd, k_even, lane_a, dk), (v_odd, v_even, lane_b, dv))
                    for odd_ref, even_ref, lane, value_grad in pairs:
                        dst = lane.index(j & ~1) * tokens + m * local_rows
                        at = (slice(dst, dst + local_rows), slice(g * head, (g + 1) * head))
                        (odd_ref if j % 2 else even_ref)[at] = value_grad[src]
        dq, gain_grad = heads_backward(ungroup(pieces), qpre[...], qg[...], cos[...], sin[...])
        dq_out[...] = dq.astype(LOW)
        gain_out[...] = gain_grad

    lane_kv = shape_of((lanes * tokens, kv_width), LOW)
    k_odd, k_even, v_odd, v_even, dq_low, dg_low, branch_rows, grad_qgain = run_kernel(
        back_body,
        [
            lane_kv,
            lane_kv,
            lane_kv,
            lane_kv,
            shape_of((tokens, q_width), LOW),
            shape_of((tokens, q_width), LOW),
            shape_of((tokens, width), LOW),
            shape_of((1, head), F32),
        ],
        [
            query_low,
            query_pre,
            gate_pre,
            attended,
            cosine,
            sine,
            q_gain,
            query_pos,
            key_pos,
            *keys,
            *values,
            *w_o,
            branch_grad,
        ],
        5 * att_flops // 2 + 2 * tokens * width * q_width,
    )
    gates_last = last_steps(gates, 1, dq_low)
    ups_last = last_steps(ups, 0, dq_low)
    key_grad = scatter_lanes(join_lanes(k_even, k_odd), back_a)
    value_grad = scatter_lanes(join_lanes(v_even, v_odd), back_b)

    def write_lanes(value, odd_ref, even_ref, lane):
        for j in range(n):
            place = lane.index(j & ~1)
            at = slice(place * block, (place + 1) * block)
            (odd_ref if j % 2 else even_ref)[at] = value[j * block : (j + 1) * block].astype(LOW)

    lane_w = shape_of((lanes * block, q_width), LOW)

    def weight_body(normed_ref, dq, dg, bg, gated, *refs):
        wq, wg, outs = split_refs(refs, steps, steps)
        g_odd, g_even, o_odd, o_even, q_odd, q_even, acc = outs
        low = normed_ref[...]
        write_lanes(dot_tn(low, dg[...]), g_odd, g_even, lane_a)
        write_lanes(dot_tn(bg[...], gated[...]), o_odd, o_even, lane_b)
        write_lanes(dot_tn(low, dq[...]), q_odd, q_even, lane_a)
        acc[...] = dot_nt(dq[...], rows_of(wq, q_place)) + dot_nt(dg[...], rows_of(wg, g_place))

    g_odd, g_even, o_odd, o_even, q_odd, q_even, normed_acc = run_kernel(
        weight_body,
        [lane_w] * 6 + [shape_of((tokens, width), F32)],
        [after(normed, down_raw), dq_low, dg_low, branch_rows, gated_low, *w_q, *w_g],
        10 * tokens * width * q_width,
    )

    def key_body(dk, dv, kpre, cos, sin, kg, normed_ref, acc, *refs):
        wkv, (kv_odd, kv_even, gain_out, send_out) = split_refs(refs, steps)
        dkey, gain_grad = heads_backward(
            dk[...] * scale, kpre[...], kg[...], cos[...], sin[...]
        )
        gain_out[...] = gain_grad
        low = jnp.concatenate([dkey.astype(LOW), dv[...].astype(LOW)], axis=1)
        write_blocks(acc[...] + dot_nt(low, rows_of(wkv, kv_place)), send_out)
        write_lanes(dot_tn(normed_ref[...], low), kv_odd, kv_even, lane_b)

    lane_w2 = shape_of((lanes * block, 2 * kv_width), LOW)
    kv_odd, kv_even, grad_kgain, send = run_kernel(
        key_body,
        [lane_w2, lane_w2, shape_of((1, head), F32), block_out],
        [key_grad, value_grad, key_pre, cosine, sine, k_gain, normed, normed_acc, *w_kv],
        8 * tokens * width * kv_width,
    )
    gate_raw, grad_hgate = return_units(gates_last, down_raw)
    got = exchange_tp(after(send, gate_raw))
    _, grad_hup = return_units(ups_last, got)
    ready = (key_grad, value_grad)
    g_odd, o_odd, q_odd = after((g_odd, o_odd, q_odd), *ready)
    grad_gating = scatter_lanes(join_lanes(g_even, g_odd), back_a)
    grad_outproj = scatter_lanes(join_lanes(o_even, o_odd), back_b).T
    grad_query = scatter_lanes(join_lanes(q_even, q_odd), back_a)
    grad_kv = scatter_lanes(join_lanes(kv_even, kv_odd), back_b)

    def input_body(me_ref, x, gain, mg, got_ref, in_out, gain_out, total_ref):
        total_ref[...] = sum_blocks(got_ref)
        total = read_permuted(total_ref, me_ref)
        rows = x[...]
        r = inverse_rms(rows)
        unit = rows * r
        gain_out[...] = jnp.sum(total * unit, axis=0, keepdims=True)
        u = total * gain[...]
        in_out[...] = mg[...] + r * (u - unit * jnp.mean(u * unit, -1, keepdims=True))

    input_grad, grad_first = run_part(
        input_body,
        [part_f32, gain_f32],
        [x_part, first_gain[None], middle_grad, outer_permute(got)],
    )
    gains = jnp.concatenate([grad_first, grad_second, grad_qgain, grad_kgain], axis=1)
    gains = gains.reshape(-1, head)
    for mask in [1 << b for b in range((p - 1).bit_length())]:
        gains = gains + swap(gains, "tp", mask)
    for mask in masks:
        gains = gains + swap(gains, "seq", mask)
    gains = gains.reshape(-1)

    ffn_out = tree_sum([out_got[b].astype(F32) for b in range(p)])
    layer_rows = (middle + ffn_out).astype(LOW)

    grad_hgate = grad_hgate.T
    grad_hup = grad_hup.T
    return (
        layer_rows.reshape(micros, part, width),
        input_grad.reshape(micros, part, width),
        gains[:width],
        grad_query,
        grad_kv[:, :kv_width],
        grad_kv[:, kv_width:],
        grad_gating,
        grad_outproj,
        gains[2 * width : 2 * width + head],
        gains[2 * width + head :],
        gains[width : 2 * width],
        grad_hgate,
        grad_hup,
        grad_hdown,
    )


def solution(mesh):
    in_specs = (
        P(None, "seq", None),
        P(None, "seq"),
        P(),
        P("seq", "tp"),
        P("seq", "tp"),
        P("seq", "tp"),
        P("seq", "tp"),
        P("tp", "seq"),
        P(),
        P(),
        P(),
        P("tp", "seq"),
        P("tp", "seq"),
        P("seq", "tp"),
        P(None, ("seq", "tp"), None),
    )
    out_specs = (
        P(None, ("seq", "tp"), None),
        P(None, ("seq", "tp"), None),
        P(),
        P("seq", "tp"),
        P("seq", "tp"),
        P("seq", "tp"),
        P("seq", "tp"),
        P("tp", "seq"),
        P(),
        P(),
        P(),
        P("tp", "seq"),
        P("tp", "seq"),
        P("seq", "tp"),
    )
    return jax.shard_map(
        per_device, mesh=mesh, in_specs=in_specs, out_specs=out_specs, check_vma=False
    )
```

```python
import jax
import jax.numpy as jnp
from jax import lax
from jax.experimental import pallas as pl
from jax.experimental.pallas import tpu as pltpu
from jax.sharding import PartitionSpec as P

EPS = 1e-06
ROPE_BASE = 5000000.0
NEG_LARGE = -1e30
F32 = jnp.float32
LOW = jnp.bfloat16
VMEM_LIMIT = 60 * 1024 * 1024


def shape_of(shape, dtype):
    return jax.ShapeDtypeStruct(shape, dtype)


def run_kernel(body, outs, args, flops, scalars=None):
    moved = sum(a.size * a.dtype.itemsize for a in args)
    moved += sum(o.size * o.dtype.itemsize for o in outs)
    specs = [pl.BlockSpec(memory_space=pltpu.VMEM)] * len(args)
    if scalars is not None:
        specs = [pl.BlockSpec(memory_space=pltpu.SMEM)] + specs
        args = [scalars] + list(args)
    return pl.pallas_call(
        body,
        out_shape=outs,
        in_specs=specs,
        out_specs=[pl.BlockSpec(memory_space=pltpu.VMEM)] * len(outs),
        compiler_params=pltpu.CompilerParams(vmem_limit_bytes=VMEM_LIMIT),
        cost_estimate=pl.CostEstimate(
            flops=flops // 8, transcendentals=0, bytes_accessed=moved // 8
        ),
    )(*args)


def dot_nn(left, right):
    return jnp.dot(left, right, preferred_element_type=F32)


def dot_nt(left, right):
    return lax.dot_general(left, right, (((1,), (1,)), ((), ())), preferred_element_type=F32)


def dot_tn(left, right):
    return lax.dot_general(left, right, (((0,), (0,)), ((), ())), preferred_element_type=F32)


def rows_of(refs, place):
    return jnp.concatenate([refs[i][e] for i, e in (place[s] for s in range(len(place)))], axis=0)


def swap(value, axis, mask):
    count = lax.axis_size(axis)
    return lax.ppermute(value, axis, [(i, i ^ mask) for i in range(count)])


def gather_pieces(value, axis, order, hold=None, hold_last=None):
    pieces, place, slots = [value[None]], {0: (0, 0)}, [0]
    for mask in order[:-1]:
        sent = pieces[0] if len(pieces) == 1 else jnp.concatenate(pieces)
        if hold is not None and len(pieces) == 2:
            sent = after(sent, hold)
        last = slots
        pieces.append(swap(sent, axis, mask))
        got = [s ^ mask for s in slots]
        place.update({s: (len(pieces) - 1, i) for i, s in enumerate(got)})
        slots = slots + got
    received = pieces[-1] if hold_last is None else after(pieces[-1], hold_last)
    for piece, ids in ((sent, last), (received, got)):
        pieces.append(swap(piece, axis, order[-1]))
        place.update({s ^ order[-1]: (len(pieces) - 1, i) for i, s in enumerate(ids)})
    return pieces, place


def lane_order(order):
    return sorted(range(0, 2 << len(order), 2), key=lambda s: [s & mask for mask in order])


def sum_halves(keep, got, last):
    if last:
        return keep.astype(F32) + got.astype(F32)
    half = keep.shape[0] // 2
    sides = (slice(None, half), slice(half, None))
    return tuple((keep[at].astype(F32) + got[at].astype(F32)).astype(LOW) for at in sides)


def join_lanes(keep, send, last=False):
    return sum_halves(keep, swap(send, "seq", 1), last)


def scatter_step(halves, mask, last, hold=None):
    keep, send = halves
    got = swap(send, "seq", mask)
    if hold is not None:
        got = after(got, hold)
    return sum_halves(keep, got, last)


def scatter_lanes(total, order, hold=None):
    for mask in order:
        total = scatter_step(total, mask, mask == order[-1], hold if mask == order[0] else None)
    return total


def exchange_tp(blocks):
    return lax.all_to_all(blocks, "tp", 0, 0, tiled=True)


def spread_tp(value):
    count = lax.axis_size("tp")
    return exchange_tp(jnp.broadcast_to(value[None], (count,) + value.shape))


def after(value, *earlier):
    return lax.optimization_barrier((value, earlier))[0]


def tree_sum(terms):
    while len(terms) > 1:
        terms = [terms[i] + terms[i + 1] for i in range(0, len(terms), 2)]
    return terms[0]


def inverse_rms(value):
    return lax.rsqrt(jnp.mean(value * value, axis=-1, keepdims=True) + EPS)


def per_device(
    layer_in,
    positions,
    first_gain,
    query_proj,
    key_projection,
    value_projection,
    gate_proj,
    output_proj,
    query_gain,
    key_norm_gain,
    second_gain,
    hidden_gate,
    hidden_up,
    hidden_down,
    out_cotangent,
):
    micros, local_rows, width = layer_in.shape
    head = query_gain.shape[0]
    n = lax.axis_size("seq")
    p = lax.axis_size("tp")
    me_seq = lax.axis_index("seq")
    me_tp = lax.axis_index("tp")
    me = jnp.stack([me_seq, me_tp]).astype(jnp.int32)
    part = local_rows // p
    tokens = micros * local_rows
    ptok = micros * part
    block = width // n
    chunk = width // p
    q_width = query_proj.shape[1]
    kv_width = key_projection.shape[1]
    q_heads = q_width // head
    kv_heads = kv_width // head
    group = q_heads // kv_heads
    units = hidden_down.shape[0] // p
    half_a = units // 2 // 16 * 16
    half_b = units - half_a
    total_rows = local_rows * n
    scale = head ** (-0.5)
    masks = [1 << b for b in range((n - 1).bit_length())]
    go_a = masks[1:] + masks[:1]
    go_b = masks[:0:-1] + masks[:1]
    back_a = masks[1:]
    back_b = masks[:0:-1]
    even = list(range(0, n, 2))
    odd = list(range(1, n, 2))
    lane_a, lane_b = lane_order(back_a), lane_order(back_b)
    inner = block % 128 == 0

    def permute_columns(value):
        return jnp.concatenate(
            [
                lax.dynamic_slice_in_dim(value, (me_seq ^ j) * block, block, value.ndim - 1)
                for j in range(n)
            ],
            axis=-1,
        )

    def outer_permute(value):
        return value if inner else permute_columns(value)

    def read_permuted(ref, me_ref):
        if not inner:
            return ref[...]
        where = [pl.multiple_of((me_ref[0] ^ j) * block, block) for j in range(n)]
        return jnp.concatenate([ref[:, pl.ds(w, block)] for w in where], axis=1)

    def write_blocks(value, ref):
        for b in range(p):
            for m in range(micros):
                start = m * local_rows + b * part
                ref[b, m * part : (m + 1) * part, :] = value[start : start + part].astype(LOW)

    def read_blocks(ref):
        return jnp.concatenate(
            [ref[b, m * part : (m + 1) * part, :] for m in range(micros) for b in range(p)], axis=0
        )

    def sum_blocks(ref):
        return tree_sum([ref[b].astype(F32) for b in range(p)])

    block_out = shape_of((p, ptok, width), LOW)

    w3 = jnp.stack([hidden_gate.T, hidden_up.T, hidden_down]).reshape(3, p, units, chunk)
    w3 = w3.transpose(1, 0, 2, 3)

    w_q, q_place = gather_pieces(query_proj, "seq", go_a)
    w_kv, kv_place = gather_pieces(
        jnp.concatenate([key_projection, value_projection], axis=1), "seq", go_b
    )
    w_g, g_place = gather_pieces(gate_proj, "seq", go_a)
    w_o, o_place = gather_pieces(output_proj.T, "seq", go_b)
    steps = len(w_q)
    wire = exchange_tp(after(w3, w_q[1], w_kv[1]))
    cot_part = out_cotangent.reshape(ptok, width)
    cot = spread_tp(after(cot_part, wire)).reshape(tokens, width)

    x_part = lax.dynamic_slice_in_dim(layer_in, me_tp * part, part, 1)
    x_part = x_part.reshape(ptok, width).astype(F32)
    x_rows = outer_permute(layer_in.reshape(tokens, width))
    places = positions.reshape(tokens)
    gain_row = outer_permute(first_gain[None])
    middle_lane = head // 2
    inverse = jnp.exp(-(jnp.arange(middle_lane, dtype=F32) * 2.0 / head) * jnp.log(ROPE_BASE))
    angles = places.astype(F32)[:, None] * inverse[None, :]
    cosine = jnp.concatenate([jnp.cos(angles), jnp.cos(angles)], axis=-1)
    sine = jnp.concatenate([-jnp.sin(angles), jnp.sin(angles)], axis=-1)
    q_gain = query_gain[None]
    k_gain = key_norm_gain[None]

    def split_refs(refs, *counts):
        out = []
        for c in counts:
            out.append(refs[:c])
            refs = refs[c:]
        return out + [refs]

    def heads_forward(pre, gain, cos, sin):
        out = []
        for h in range(pre.shape[1] // head):
            u = pre[:, h * head : (h + 1) * head]
            y = u * inverse_rms(u) * gain
            out.append(y * cos + pltpu.roll(y, middle_lane, 1) * sin)
        return jnp.concatenate(out, axis=1)

    def heads_backward(grad, pre, gain, cos, sin):
        out = []
        gain_grad = jnp.zeros((1, head), F32)
        for h in range(pre.shape[1] // head):
            u = pre[:, h * head : (h + 1) * head]
            g = grad[:, h * head : (h + 1) * head]
            r = inverse_rms(u)
            unit = u * r
            y = g * cos + pltpu.roll(g * sin, middle_lane, 1)
            gain_grad = gain_grad + jnp.sum(y * unit, axis=0, keepdims=True)
            t = y * gain
            out.append(r * (t - unit * jnp.mean(t * unit, axis=-1, keepdims=True)))
        return jnp.concatenate(out, axis=1), gain_grad

    def qkv_body(me_ref, x, gain, cos, sin, qg, kg, *refs):
        wq, wkv, outs = split_refs(refs, steps, steps)
        normed_out, qpre_out, kpre_out, q_out, k_out, v_out = outs
        rows = read_permuted(x, me_ref).astype(F32)
        low = (rows * inverse_rms(rows) * read_permuted(gain, me_ref)).astype(LOW)
        normed_out[...] = low
        kv = dot_nn(low, rows_of(wkv, kv_place))
        key = kv[:, :kv_width]
        kpre_out[...] = key
        v_out[...] = kv[:, kv_width:].astype(LOW)
        k_out[...] = heads_forward(key, kg[...], cos[...], sin[...]).astype(LOW)
        query = dot_nn(low, rows_of(wq, q_place))
        qpre_out[...] = query
        q_out[...] = heads_forward(query, qg[...], cos[...], sin[...]).astype(LOW)

    normed, query_pre, key_pre, query_low, key_low, value_low = run_kernel(
        qkv_body,
        [
            shape_of((tokens, width), LOW),
            shape_of((tokens, q_width), F32),
            shape_of((tokens, kv_width), F32),
            shape_of((tokens, q_width), LOW),
            shape_of((tokens, kv_width), LOW),
            shape_of((tokens, kv_width), LOW),
        ],
        [after(x_rows, w_g[1], w_o[1]), gain_row, cosine, sine, q_gain, k_gain, *w_q, *w_kv],
        2 * tokens * width * (q_width + 2 * kv_width),
        me,
    )
    keys, key_place = gather_pieces(key_low, "seq", go_a)
    values, value_place = gather_pieces(value_low, "seq", go_b)

    f_own = wire.transpose(1, 2, 0, 3).reshape(3, units, width)
    f_own = after(f_own, keys[-1], values[-1], w_g[-1], w_o[-1])

    inside = jnp.arange(local_rows, dtype=jnp.int32)
    query_pos = jnp.tile(me_seq * local_rows + inside, group)[:, None]
    key_pos = jnp.concatenate([(me_seq ^ j) * local_rows + inside for j in range(n)])[None, :]

    def group_rows(value, m, g):
        rows = value[m * local_rows : (m + 1) * local_rows]
        heads = range(g * group, (g + 1) * group)
        return jnp.concatenate([rows[:, h * head : (h + 1) * head] for h in heads], axis=0)

    def slot_rows(refs, place, m, g):
        rows = []
        for j in range(n):
            index, entry = place[j]
            start = m * local_rows
            at = (entry, slice(start, start + local_rows), slice(g * head, (g + 1) * head))
            rows.append(refs[index][at])
        return jnp.concatenate(rows, axis=0)

    def softmax_of(query, key, qpos, kpos):
        scores = jnp.where(kpos <= qpos, dot_nt(query, key) * scale, NEG_LARGE)
        weights = jnp.exp(scores - jnp.max(scores, axis=-1, keepdims=True))
        return weights * (1.0 / jnp.sum(weights, axis=-1, keepdims=True))

    def ungroup(pieces):
        rows = []
        for m in range(micros):
            columns = []
            for g in range(kv_heads):
                value = pieces[m, g]
                columns += [
                    value[h * local_rows : (h + 1) * local_rows] for h in range(group)
                ]
            rows.append(jnp.concatenate(columns, axis=1))
        return jnp.concatenate(rows, axis=0)

    def attend_body(q, normed_ref, qpos, kpos, *refs):
        ks, vs, wg, wo, outs = split_refs(refs, steps, steps, steps, steps)
        gate_out, att_out, gated_out, send_out = outs
        gate = dot_nn(normed_ref[...], rows_of(wg, g_place))
        gate_out[...] = gate
        query = q[...]
        pieces = {}
        for m in range(micros):
            for g in range(kv_heads):
                prob = softmax_of(
                    group_rows(query, m, g), slot_rows(ks, key_place, m, g), qpos[...], kpos[...]
                )
                pieces[m, g] = dot_nn(prob.astype(LOW), slot_rows(vs, value_place, m, g))
        att = ungroup(pieces)
        att_out[...] = att
        gated = (att * jax.nn.sigmoid(gate)).astype(LOW)
        gated_out[...] = gated
        write_blocks(dot_nt(gated, rows_of(wo, o_place)), send_out)

    att_flops = 4 * tokens * total_rows * q_width
    gate_pre, attended, gated_low, send = run_kernel(
        attend_body,
        [
            shape_of((tokens, q_width), F32),
            shape_of((tokens, q_width), F32),
            shape_of((tokens, q_width), LOW),
            block_out,
        ],
        [after(query_low, wire), normed, query_pos, key_pos, *keys, *values, *w_g, *w_o],
        att_flops + 4 * tokens * width * q_width,
    )
    got = exchange_tp(after(send, cot))

    def middle_body(me_ref, x, gain, got_ref, middle_out, low_out, total_ref):
        total_ref[...] = sum_blocks(got_ref)
        rows = x[...] + read_permuted(total_ref, me_ref)
        middle_out[...] = rows
        low = (rows * inverse_rms(rows) * gain[...]).astype(LOW)
        for b in range(p):
            low_out[b] = low

    def run_part(body, outs, args):
        specs = [pl.BlockSpec(memory_space=pltpu.SMEM)]
        specs += [pl.BlockSpec(memory_space=pltpu.VMEM)] * len(args)
        return pl.pallas_call(
            body,
            out_shape=outs,
            in_specs=specs,
            out_specs=[pl.BlockSpec(memory_space=pltpu.VMEM)] * len(outs),
            scratch_shapes=[pltpu.VMEM((ptok, width), F32)],
            compiler_params=pltpu.CompilerParams(vmem_limit_bytes=VMEM_LIMIT),
            cost_estimate=pl.CostEstimate(
                flops=20 * ptok * width, transcendentals=0, bytes_accessed=20 * ptok * width
            ),
        )(me, *args)

    part_f32 = shape_of((ptok, width), F32)
    gain_f32 = shape_of((1, width), F32)
    second = second_gain[None]
    middle, normed_two = run_part(
        middle_body,
        [part_f32, block_out],
        [x_part, second, outer_permute(got)],
    )
    n2 = exchange_tp(normed_two).reshape(tokens, width)
    f_a, fa_place = gather_pieces(f_own[:, :half_a], "seq", go_a, send, n2)
    f_b, fb_place = gather_pieces(f_own[:, half_a:], "seq", go_b, send, n2)

    lanes = n // 2
    halves = (half_a, half_b)
    lane_units = lanes * units
    pair = 2 if lanes % 2 == 0 else 1
    anywhere = pl.BlockSpec(memory_space=pl.ANY)
    whole = pl.BlockSpec(memory_space=pltpu.VMEM)
    f_places = (fa_place, fb_place)

    def start_loads(slots, refs, skipped, w, sem):
        count = len(refs) // 2
        loads = []
        for s, slot in enumerate(slots):
            for t in range(2):
                index, entry = f_places[t][slot]
                where = pl.ds(s * units + t * half_a, halves[t])
                source = refs[t * count + index - skipped].at[entry]
                copy = pltpu.make_async_copy(source, w.at[:, where, :], sem.at[2 * s + t])
                copy.start()
                loads.append(copy)
        return loads

    def pair_rows(step, loads):
        for copy in loads[2 * pair * step : 2 * pair * (step + 1)]:
            copy.wait()
        return slice(step * pair * units, (step + 1) * pair * units)

    def forward_body(last, slots, count, x, *refs):
        held, before, outs, (w, sem) = split_refs(refs, 2 * count, 1 if last else 0, 4)
        loads = start_loads(slots, held, steps - 2 if last else 0, w, sem)
        for step in range(lanes // pair):
            rows = pair_rows(step, loads)
            gate = dot_nt(w[0, rows], x[...])
            up = dot_nt(w[1, rows], x[...])
            outs[0][rows] = gate
            outs[1][rows] = up
            outs[2][rows] = (gate * jax.nn.sigmoid(gate) * up).astype(LOW)
        out = dot_tn(outs[2][...], w[2])
        if last:
            out = out + before[0][...]
        outs[3][...] = out.astype(outs[3].dtype)

    def run_forward(last, dtype, slots, *before):
        use = slice(steps - 2, steps) if last else slice(0, steps - 2)
        held = [*f_a[use], *f_b[use]]
        return pl.pallas_call(
            lambda *r: forward_body(last, slots, len(held) // 2, *r),
            out_shape=[
                shape_of((lane_units, tokens), F32),
                shape_of((lane_units, tokens), F32),
                shape_of((lane_units, tokens), LOW),
                shape_of((tokens, width), dtype),
            ],
            in_specs=[whole] + [anywhere] * len(held) + [whole] * len(before),
            out_specs=[whole] * 4,
            scratch_shapes=[
                pltpu.VMEM((3, lane_units, width), LOW),
                pltpu.SemaphoreType.DMA((2 * lanes,)),
            ],
            compiler_params=pltpu.CompilerParams(vmem_limit_bytes=VMEM_LIMIT),
            cost_estimate=pl.CostEstimate(
                flops=6 * tokens * width * lane_units // 8,
                transcendentals=0,
                bytes_accessed=(6 * lane_units * width + 4 * tokens * width) // 8,
            ),
        )(n2, *held, *before)

    *acts_even, out_even = run_forward(False, F32, even)
    *acts_odd, out_sum = run_forward(True, LOW, odd, out_even)
    out_got = exchange_tp(out_sum.reshape(p, ptok, width))

    def backward_body(first, slots, count, x, c, gate_ref, up_ref, hid_ref, *refs):
        held, before, grads, (acc,), scratch = split_refs(
            refs, 2 * count, 0 if first else 1, 6, 1
        )
        w, low = scratch[:2]
        gbufs, in_sem, out_sem = scratch[2:8], scratch[8], scratch[9]
        loads = start_loads(slots, held, steps - 2 if first else 0, w, in_sem)
        stores = []

        def store(k, step, value):
            t, h = k % 2, halves[k % 2]
            for q in range(pair):
                slot = slots[step * pair + q] & ~1
                start = (lane_a, lane_b)[t].index(slot) * h
                at = pl.ds(start, h)
                source = q * units + t * half_a
                gbufs[k][start : start + h] = value[source : source + h]
                copy = pltpu.make_async_copy(
                    gbufs[k].at[at], grads[k].at[at], out_sem.at[6 * (step * pair + q) + k]
                )
                copy.start()
                stores.append(copy)

        for step in range(lanes // pair):
            rows = pair_rows(step, loads)
            gate, up = gate_ref[rows], up_ref[rows]
            grad = dot_nt(w[2, rows], c[...])
            sig = jax.nn.sigmoid(gate)
            gate_grad = (grad * up * sig * (1.0 + gate * (1.0 - sig))).astype(LOW)
            up_grad = (grad * gate * sig).astype(LOW)
            low[0, rows] = gate_grad
            low[1, rows] = up_grad
            sides = ((hid_ref[rows], c), (gate_grad, x), (up_grad, x))
            for i, (left, right) in zip((2, 0, 1), sides):
                value = dot_nn(left, right[...]).astype(LOW)
                store(2 * i, step, value)
                store(2 * i + 1, step, value)
        back = dot_tn(low[0], w[0]) + dot_tn(low[1], w[1])
        if not first:
            back = back + before[0][...]
        acc[...] = back.astype(acc.dtype)
        for copy in stores:
            copy.wait()

    def run_backward(first, dtype, slots, acts, *before):
        grad_outs = [shape_of((lanes * h, width), LOW) for _ in range(3) for h in halves]
        use = slice(steps - 2, steps) if first else slice(0, steps - 2)
        held = [*f_a[use], *f_b[use]]
        return pl.pallas_call(
            lambda *r: backward_body(first, slots, len(held) // 2, *r),
            out_shape=grad_outs + [shape_of((tokens, width), dtype)],
            in_specs=[whole] * 5 + [anywhere] * len(held) + [whole] * len(before),
            out_specs=[anywhere] * 6 + [whole],
            scratch_shapes=[
                pltpu.VMEM((3, lane_units, width), LOW),
                pltpu.VMEM((2, lane_units, tokens), LOW),
                *[pltpu.VMEM((lanes * h, width), LOW) for _ in range(3) for h in halves],
                pltpu.SemaphoreType.DMA((2 * lanes,)),
                pltpu.SemaphoreType.DMA((6 * lanes,)),
            ],
            compiler_params=pltpu.CompilerParams(vmem_limit_bytes=VMEM_LIMIT),
            cost_estimate=pl.CostEstimate(
                flops=12 * tokens * width * lane_units // 8,
                transcendentals=0,
                bytes_accessed=(12 * lane_units * width + 8 * tokens * width) // 8,
            ),
        )(n2, cot, *acts, *held, *before)

    *f_odd, back_odd = run_backward(True, F32, odd, acts_odd)
    *f_even, back_sum = run_backward(False, LOW, even, acts_even, back_odd)
    back_got = exchange_tp(after(back_sum, out_got).reshape(p, ptok, width))
    orders = (back_a, back_b)

    def first_steps(index):
        return [join_lanes(f_even[2 * index + t], f_odd[2 * index + t]) for t in range(2)]

    def next_steps(states, level, hold=None):
        last = level == len(back_a) - 1
        return [
            scatter_step(state, orders[t][level], last, hold) for t, state in enumerate(states)
        ]

    def last_steps(states, level, hold=None):
        for k in range(level, len(back_a)):
            states = next_steps(states, k, hold)
        return states

    def return_units(states, hold):
        blocks = jnp.concatenate(states).astype(LOW)
        blocks = blocks.reshape(units, p, chunk).transpose(1, 0, 2)
        raw = exchange_tp(after(blocks, hold))
        return raw, raw.reshape(p * units, chunk).astype(F32)

    down, gates, ups = first_steps(2), first_steps(0), first_steps(1)
    down = next_steps(down, 0)

    def branch_body(me_ref, mid, cot_ref, gain, got_ref, mg_out, low_out, gain_out, scratch):
        total = sum_blocks(got_ref)
        rows = mid[...]
        r = inverse_rms(rows)
        unit = rows * r
        gain_out[...] = jnp.sum(total * unit, axis=0, keepdims=True)
        u = total * gain[...]
        grad = cot_ref[...].astype(F32) + r * (u - unit * jnp.mean(u * unit, -1, keepdims=True))
        mg_out[...] = grad
        scratch[...] = grad
        low = read_permuted(scratch, me_ref).astype(LOW)
        for b in range(p):
            low_out[b] = low

    middle_grad, branch_low, grad_second = run_part(
        branch_body,
        [part_f32, block_out, gain_f32],
        [middle, cot_part, second, back_got],
    )
    branch_grad = exchange_tp(outer_permute(branch_low))
    gates = next_steps(gates, 0, branch_low)
    ups = [after(u, *down) for u in ups]
    down_last = last_steps(down, 1, branch_low)
    down_raw, grad_hdown = return_units(down_last, branch_grad)

    def back_body(q, qpre, gate, att, cos, sin, qg, qpos, kpos, *refs):
        ks, vs, wo, (bg,), outs = split_refs(refs, steps, steps, steps, 1)
        k_odd, k_even, v_odd, v_even, dq_out, dg_out, bg_out, gain_out = outs
        branch = read_blocks(bg)
        bg_out[...] = branch
        gated_grad = dot_nn(branch, rows_of(wo, o_place))
        sig = jax.nn.sigmoid(gate[...])
        att_grad = (gated_grad * sig).astype(LOW)
        dg_out[...] = (gated_grad * att[...] * sig * (1.0 - sig)).astype(LOW)
        product = att_grad.astype(F32) * att[...]
        query = q[...]
        pieces = {}
        for m in range(micros):
            for g in range(kv_heads):
                qr = group_rows(query, m, g)
                ag = group_rows(att_grad, m, g)
                key = slot_rows(ks, key_place, m, g)
                value = slot_rows(vs, value_place, m, g)
                delta = jnp.sum(group_rows(product, m, g), axis=-1, keepdims=True)
                prob = softmax_of(qr, key, qpos[...], kpos[...])
                ds = (prob * (dot_nt(ag, value) - delta)).astype(LOW)
                pieces[m, g] = dot_nn(ds, key) * scale
                dk = dot_tn(ds, qr).astype(LOW)
                dv = dot_tn(prob.astype(LOW), ag).astype(LOW)
                for j in range(n):
                    src = slice(j * local_rows, (j + 1) * local_rows)
                    pairs = ((k_odd, k_even, lane_a, dk), (v_odd, v_even, lane_b, dv))
                    for odd_ref, even_ref, lane, value_grad in pairs:
                        dst = lane.index(j & ~1) * tokens + m * local_rows
                        at = (slice(dst, dst + local_rows), slice(g * head, (g + 1) * head))
                        (odd_ref if j % 2 else even_ref)[at] = value_grad[src]
        dq, gain_grad = heads_backward(ungroup(pieces), qpre[...], qg[...], cos[...], sin[...])
        dq_out[...] = dq.astype(LOW)
        gain_out[...] = gain_grad

    lane_kv = shape_of((lanes * tokens, kv_width), LOW)
    k_odd, k_even, v_odd, v_even, dq_low, dg_low, branch_rows, grad_qgain = run_kernel(
        back_body,
        [
            lane_kv,
            lane_kv,
            lane_kv,
            lane_kv,
            shape_of((tokens, q_width), LOW),
            shape_of((tokens, q_width), LOW),
            shape_of((tokens, width), LOW),
            shape_of((1, head), F32),
        ],
        [
            query_low,
            query_pre,
            gate_pre,
            attended,
            cosine,
            sine,
            q_gain,
            query_pos,
            key_pos,
            *keys,
            *values,
            *w_o,
            branch_grad,
        ],
        5 * att_flops // 2 + 2 * tokens * width * q_width,
    )
    key_halves = join_lanes(k_even, k_odd)
    value_halves = join_lanes(v_even, v_odd)
    gates_last = last_steps(gates, 1, (key_halves, value_halves))
    ups_last = last_steps(ups, 0, (key_halves, value_halves))
    key_grad = scatter_lanes(key_halves, back_a, down_raw)
    value_grad = scatter_lanes(value_halves, back_b, down_raw)

    def write_lanes(value, odd_ref, even_ref, lane):
        for j in range(n):
            place = lane.index(j & ~1)
            at = slice(place * block, (place + 1) * block)
            (odd_ref if j % 2 else even_ref)[at] = value[j * block : (j + 1) * block].astype(LOW)

    lane_w = shape_of((lanes * block, q_width), LOW)

    def weight_body(normed_ref, dq, dg, bg, gated, *refs):
        wq, wg, outs = split_refs(refs, steps, steps)
        g_odd, g_even, o_odd, o_even, q_odd, q_even, acc = outs
        low = normed_ref[...]
        write_lanes(dot_tn(low, dg[...]), g_odd, g_even, lane_a)
        write_lanes(dot_tn(bg[...], gated[...]), o_odd, o_even, lane_b)
        write_lanes(dot_tn(low, dq[...]), q_odd, q_even, lane_a)
        acc[...] = dot_nt(dq[...], rows_of(wq, q_place)) + dot_nt(dg[...], rows_of(wg, g_place))

    g_odd, g_even, o_odd, o_even, q_odd, q_even, normed_acc = run_kernel(
        weight_body,
        [lane_w] * 6 + [shape_of((tokens, width), F32)],
        [after(normed, down_raw), dq_low, dg_low, branch_rows, gated_low, *w_q, *w_g],
        10 * tokens * width * q_width,
    )

    def key_body(dk, dv, kpre, cos, sin, kg, normed_ref, acc, *refs):
        wkv, (kv_odd, kv_even, gain_out, send_out) = split_refs(refs, steps)
        dkey, gain_grad = heads_backward(
            dk[...] * scale, kpre[...], kg[...], cos[...], sin[...]
        )
        gain_out[...] = gain_grad
        low = jnp.concatenate([dkey.astype(LOW), dv[...].astype(LOW)], axis=1)
        write_blocks(acc[...] + dot_nt(low, rows_of(wkv, kv_place)), send_out)
        write_lanes(dot_tn(normed_ref[...], low), kv_odd, kv_even, lane_b)

    lane_w2 = shape_of((lanes * block, 2 * kv_width), LOW)
    kv_odd, kv_even, grad_kgain, send = run_kernel(
        key_body,
        [lane_w2, lane_w2, shape_of((1, head), F32), block_out],
        [key_grad, value_grad, key_pre, cosine, sine, k_gain, normed, normed_acc, *w_kv],
        8 * tokens * width * kv_width,
    )
    gate_raw, grad_hgate = return_units(gates_last, down_raw)
    got = exchange_tp(after(send, gate_raw))
    _, grad_hup = return_units(ups_last, got)
    ready = (key_grad, value_grad)
    g_odd, o_odd, q_odd = after((g_odd, o_odd, q_odd), *ready)
    grad_gating = scatter_lanes(join_lanes(g_even, g_odd), back_a)
    grad_outproj = scatter_lanes(join_lanes(o_even, o_odd), back_b).T
    grad_query = scatter_lanes(join_lanes(q_even, q_odd), back_a, got)
    grad_kv = scatter_lanes(join_lanes(kv_even, kv_odd), back_b, got)

    def input_body(me_ref, x, gain, mg, got_ref, in_out, gain_out, total_ref):
        total_ref[...] = sum_blocks(got_ref)
        total = read_permuted(total_ref, me_ref)
        rows = x[...]
        r = inverse_rms(rows)
        unit = rows * r
        gain_out[...] = jnp.sum(total * unit, axis=0, keepdims=True)
        u = total * gain[...]
        in_out[...] = mg[...] + r * (u - unit * jnp.mean(u * unit, -1, keepdims=True))

    input_grad, grad_first = run_part(
        input_body,
        [part_f32, gain_f32],
        [x_part, first_gain[None], middle_grad, outer_permute(got)],
    )
    gains = jnp.concatenate([grad_first, grad_second, grad_qgain, grad_kgain], axis=1)
    gains = gains.reshape(-1, head)
    for mask in [1 << b for b in range((p - 1).bit_length())]:
        gains = gains + swap(gains, "tp", mask)
    for mask in masks:
        gains = gains + swap(gains, "seq", mask)
    gains = gains.reshape(-1)

    ffn_out = tree_sum([out_got[b].astype(F32) for b in range(p)])
    layer_rows = (middle + ffn_out).astype(LOW)

    grad_hgate = grad_hgate.T
    grad_hup = grad_hup.T
    return (
        layer_rows.reshape(micros, part, width),
        input_grad.reshape(micros, part, width),
        gains[:width],
        grad_query,
        grad_kv[:, :kv_width],
        grad_kv[:, kv_width:],
        grad_gating,
        grad_outproj,
        gains[2 * width : 2 * width + head],
        gains[2 * width + head :],
        gains[width : 2 * width],
        grad_hgate,
        grad_hup,
        grad_hdown,
    )


def solution(mesh):
    in_specs = (
        P(None, "seq", None),
        P(None, "seq"),
        P(),
        P("seq", "tp"),
        P("seq", "tp"),
        P("seq", "tp"),
        P("seq", "tp"),
        P("tp", "seq"),
        P(),
        P(),
        P(),
        P("tp", "seq"),
        P("tp", "seq"),
        P("seq", "tp"),
        P(None, ("seq", "tp"), None),
    )
    out_specs = (
        P(None, ("seq", "tp"), None),
        P(None, ("seq", "tp"), None),
        P(),
        P("seq", "tp"),
        P("seq", "tp"),
        P("seq", "tp"),
        P("seq", "tp"),
        P("tp", "seq"),
        P(),
        P(),
        P(),
        P("tp", "seq"),
        P("tp", "seq"),
        P("seq", "tp"),
    )
    return jax.shard_map(
        per_device, mesh=mesh, in_specs=in_specs, out_specs=out_specs, check_vma=False
    )
```

```python
import jax
import jax.numpy as jnp
from jax import lax
from jax.experimental import pallas as pl
from jax.experimental.pallas import tpu as pltpu
from jax.sharding import PartitionSpec as P

EPS = 1e-06
ROPE_BASE = 5000000.0
NEG_LARGE = -1e30
F32 = jnp.float32
LOW = jnp.bfloat16
VMEM_LIMIT = 60 * 1024 * 1024


def shape_of(shape, dtype):
    return jax.ShapeDtypeStruct(shape, dtype)


def run_kernel(body, outs, args, flops, scalars=None):
    moved = sum(a.size * a.dtype.itemsize for a in args)
    moved += sum(o.size * o.dtype.itemsize for o in outs)
    specs = [pl.BlockSpec(memory_space=pltpu.VMEM)] * len(args)
    if scalars is not None:
        specs = [pl.BlockSpec(memory_space=pltpu.SMEM)] + specs
        args = [scalars] + list(args)
    return pl.pallas_call(
        body,
        out_shape=outs,
        in_specs=specs,
        out_specs=[pl.BlockSpec(memory_space=pltpu.VMEM)] * len(outs),
        compiler_params=pltpu.CompilerParams(vmem_limit_bytes=VMEM_LIMIT),
        cost_estimate=pl.CostEstimate(
            flops=flops // 8, transcendentals=0, bytes_accessed=moved // 8
        ),
    )(*args)


def dot_nn(left, right):
    return jnp.dot(left, right, preferred_element_type=F32)


def dot_nt(left, right):
    return lax.dot_general(left, right, (((1,), (1,)), ((), ())), preferred_element_type=F32)


def dot_tn(left, right):
    return lax.dot_general(left, right, (((0,), (0,)), ((), ())), preferred_element_type=F32)


def rows_of(refs, place):
    return jnp.concatenate([refs[i][e] for i, e in (place[s] for s in range(len(place)))], axis=0)


def swap(value, axis, mask):
    count = lax.axis_size(axis)
    return lax.ppermute(value, axis, [(i, i ^ mask) for i in range(count)])


def gather_pieces(value, axis, order, hold=None, hold_last=None):
    pieces, place, slots = [value[None]], {0: (0, 0)}, [0]
    for mask in order[:-1]:
        sent = pieces[0] if len(pieces) == 1 else jnp.concatenate(pieces)
        if hold is not None and len(pieces) == 2:
            sent = after(sent, hold)
        last = slots
        pieces.append(swap(sent, axis, mask))
        got = [s ^ mask for s in slots]
        place.update({s: (len(pieces) - 1, i) for i, s in enumerate(got)})
        slots = slots + got
    received = pieces[-1] if hold_last is None else after(pieces[-1], hold_last)
    for piece, ids in ((sent, last), (received, got)):
        pieces.append(swap(piece, axis, order[-1]))
        place.update({s ^ order[-1]: (len(pieces) - 1, i) for i, s in enumerate(ids)})
    return pieces, place


def lane_order(order):
    return sorted(range(0, 2 << len(order), 2), key=lambda s: [s & mask for mask in order])


def sum_halves(keep, got, last):
    if last:
        return keep.astype(F32) + got.astype(F32)
    half = keep.shape[0] // 2
    sides = (slice(None, half), slice(half, None))
    return tuple((keep[at].astype(F32) + got[at].astype(F32)).astype(LOW) for at in sides)


def join_lanes(keep, send, last=False):
    return sum_halves(keep, swap(send, "seq", 1), last)


def scatter_step(halves, mask, last, hold=None):
    keep, send = halves
    got = swap(send, "seq", mask)
    if hold is not None:
        got = after(got, hold)
    return sum_halves(keep, got, last)


def scatter_lanes(total, order, hold=None):
    for mask in order:
        total = scatter_step(total, mask, mask == order[-1], hold if mask == order[0] else None)
    return total


def exchange_tp(blocks):
    return lax.all_to_all(blocks, "tp", 0, 0, tiled=True)


def spread_tp(value):
    count = lax.axis_size("tp")
    return exchange_tp(jnp.broadcast_to(value[None], (count,) + value.shape))


def after(value, *earlier):
    return lax.optimization_barrier((value, earlier))[0]


def tree_sum(terms):
    while len(terms) > 1:
        terms = [terms[i] + terms[i + 1] for i in range(0, len(terms), 2)]
    return terms[0]


def inverse_rms(value):
    return lax.rsqrt(jnp.mean(value * value, axis=-1, keepdims=True) + EPS)


def per_device(
    layer_in,
    positions,
    first_gain,
    query_proj,
    key_projection,
    value_projection,
    gate_proj,
    output_proj,
    query_gain,
    key_norm_gain,
    second_gain,
    hidden_gate,
    hidden_up,
    hidden_down,
    out_cotangent,
):
    micros, local_rows, width = layer_in.shape
    head = query_gain.shape[0]
    n = lax.axis_size("seq")
    p = lax.axis_size("tp")
    me_seq = lax.axis_index("seq")
    me_tp = lax.axis_index("tp")
    me = jnp.stack([me_seq, me_tp]).astype(jnp.int32)
    part = local_rows // p
    tokens = micros * local_rows
    ptok = micros * part
    block = width // n
    chunk = width // p
    q_width = query_proj.shape[1]
    kv_width = key_projection.shape[1]
    q_heads = q_width // head
    kv_heads = kv_width // head
    group = q_heads // kv_heads
    units = hidden_down.shape[0] // p
    half_a = units // 2 // 16 * 16
    half_b = units - half_a
    total_rows = local_rows * n
    scale = head ** (-0.5)
    masks = [1 << b for b in range((n - 1).bit_length())]
    go_a = masks[1:] + masks[:1]
    go_b = masks[:0:-1] + masks[:1]
    back_a = masks[1:]
    back_b = masks[:0:-1]
    even = list(range(0, n, 2))
    odd = list(range(1, n, 2))
    lane_a, lane_b = lane_order(back_a), lane_order(back_b)
    inner = block % 128 == 0

    def permute_columns(value):
        return jnp.concatenate(
            [
                lax.dynamic_slice_in_dim(value, (me_seq ^ j) * block, block, value.ndim - 1)
                for j in range(n)
            ],
            axis=-1,
        )

    def outer_permute(value):
        return value if inner else permute_columns(value)

    def read_permuted(ref, me_ref):
        if not inner:
            return ref[...]
        where = [pl.multiple_of((me_ref[0] ^ j) * block, block) for j in range(n)]
        return jnp.concatenate([ref[:, pl.ds(w, block)] for w in where], axis=1)

    def write_blocks(value, ref):
        for b in range(p):
            for m in range(micros):
                start = m * local_rows + b * part
                ref[b, m * part : (m + 1) * part, :] = value[start : start + part].astype(LOW)

    def read_blocks(ref):
        return jnp.concatenate(
            [ref[b, m * part : (m + 1) * part, :] for m in range(micros) for b in range(p)], axis=0
        )

    def sum_blocks(ref):
        return tree_sum([ref[b].astype(F32) for b in range(p)])

    block_out = shape_of((p, ptok, width), LOW)

    w3 = jnp.stack([hidden_gate.T, hidden_up.T, hidden_down]).reshape(3, p, units, chunk)
    w3 = w3.transpose(1, 0, 2, 3)

    w_q, q_place = gather_pieces(query_proj, "seq", go_a)
    w_kv, kv_place = gather_pieces(
        jnp.concatenate([key_projection, value_projection], axis=1), "seq", go_b
    )
    w_g, g_place = gather_pieces(gate_proj, "seq", go_a)
    w_o, o_place = gather_pieces(output_proj.T, "seq", go_b)
    steps = len(w_q)
    wire = exchange_tp(after(w3, w_q[1], w_kv[1]))
    cot_part = out_cotangent.reshape(ptok, width)
    cot = spread_tp(after(cot_part, wire)).reshape(tokens, width)

    x_part = lax.dynamic_slice_in_dim(layer_in, me_tp * part, part, 1)
    x_part = x_part.reshape(ptok, width).astype(F32)
    x_rows = outer_permute(layer_in.reshape(tokens, width))
    places = positions.reshape(tokens)
    gain_row = outer_permute(first_gain[None])
    middle_lane = head // 2
    inverse = jnp.exp(-(jnp.arange(middle_lane, dtype=F32) * 2.0 / head) * jnp.log(ROPE_BASE))
    angles = places.astype(F32)[:, None] * inverse[None, :]
    cosine = jnp.concatenate([jnp.cos(angles), jnp.cos(angles)], axis=-1)
    sine = jnp.concatenate([-jnp.sin(angles), jnp.sin(angles)], axis=-1)
    q_gain = query_gain[None]
    k_gain = key_norm_gain[None]

    def split_refs(refs, *counts):
        out = []
        for c in counts:
            out.append(refs[:c])
            refs = refs[c:]
        return out + [refs]

    def heads_forward(pre, gain, cos, sin):
        out = []
        for h in range(pre.shape[1] // head):
            u = pre[:, h * head : (h + 1) * head]
            y = u * inverse_rms(u) * gain
            out.append(y * cos + pltpu.roll(y, middle_lane, 1) * sin)
        return jnp.concatenate(out, axis=1)

    def heads_backward(grad, pre, gain, cos, sin):
        out = []
        gain_grad = jnp.zeros((1, head), F32)
        for h in range(pre.shape[1] // head):
            u = pre[:, h * head : (h + 1) * head]
            g = grad[:, h * head : (h + 1) * head]
            r = inverse_rms(u)
            unit = u * r
            y = g * cos + pltpu.roll(g * sin, middle_lane, 1)
            gain_grad = gain_grad + jnp.sum(y * unit, axis=0, keepdims=True)
            t = y * gain
            out.append(r * (t - unit * jnp.mean(t * unit, axis=-1, keepdims=True)))
        return jnp.concatenate(out, axis=1), gain_grad

    def qkv_body(me_ref, x, gain, cos, sin, qg, kg, *refs):
        wq, wkv, outs = split_refs(refs, steps, steps)
        normed_out, qpre_out, kpre_out, q_out, k_out, v_out = outs
        rows = read_permuted(x, me_ref).astype(F32)
        low = (rows * inverse_rms(rows) * read_permuted(gain, me_ref)).astype(LOW)
        normed_out[...] = low
        kv = dot_nn(low, rows_of(wkv, kv_place))
        key = kv[:, :kv_width]
        kpre_out[...] = key
        v_out[...] = kv[:, kv_width:].astype(LOW)
        k_out[...] = heads_forward(key, kg[...], cos[...], sin[...]).astype(LOW)
        query = dot_nn(low, rows_of(wq, q_place))
        qpre_out[...] = query
        q_out[...] = heads_forward(query, qg[...], cos[...], sin[...]).astype(LOW)

    normed, query_pre, key_pre, query_low, key_low, value_low = run_kernel(
        qkv_body,
        [
            shape_of((tokens, width), LOW),
            shape_of((tokens, q_width), F32),
            shape_of((tokens, kv_width), F32),
            shape_of((tokens, q_width), LOW),
            shape_of((tokens, kv_width), LOW),
            shape_of((tokens, kv_width), LOW),
        ],
        [after(x_rows, w_g[1], w_o[1]), gain_row, cosine, sine, q_gain, k_gain, *w_q, *w_kv],
        2 * tokens * width * (q_width + 2 * kv_width),
        me,
    )
    keys, key_place = gather_pieces(key_low, "seq", go_a)
    values, value_place = gather_pieces(value_low, "seq", go_b)

    f_own = wire.transpose(1, 2, 0, 3).reshape(3, units, width)
    f_own = after(f_own, keys[-1], values[-1], w_g[-1], w_o[-1])

    inside = jnp.arange(local_rows, dtype=jnp.int32)
    query_pos = jnp.tile(me_seq * local_rows + inside, group)[:, None]
    key_pos = jnp.concatenate([(me_seq ^ j) * local_rows + inside for j in range(n)])[None, :]

    def group_rows(value, m, g):
        rows = value[m * local_rows : (m + 1) * local_rows]
        heads = range(g * group, (g + 1) * group)
        return jnp.concatenate([rows[:, h * head : (h + 1) * head] for h in heads], axis=0)

    def slot_rows(refs, place, m, g):
        rows = []
        for j in range(n):
            index, entry = place[j]
            start = m * local_rows
            at = (entry, slice(start, start + local_rows), slice(g * head, (g + 1) * head))
            rows.append(refs[index][at])
        return jnp.concatenate(rows, axis=0)

    def softmax_of(query, key, qpos, kpos):
        scores = jnp.where(kpos <= qpos, dot_nt(query, key) * scale, NEG_LARGE)
        weights = jnp.exp(scores - jnp.max(scores, axis=-1, keepdims=True))
        return weights * (1.0 / jnp.sum(weights, axis=-1, keepdims=True))

    def ungroup(pieces):
        rows = []
        for m in range(micros):
            columns = []
            for g in range(kv_heads):
                value = pieces[m, g]
                columns += [
                    value[h * local_rows : (h + 1) * local_rows] for h in range(group)
                ]
            rows.append(jnp.concatenate(columns, axis=1))
        return jnp.concatenate(rows, axis=0)

    def attend_body(q, normed_ref, qpos, kpos, *refs):
        ks, vs, wg, wo, outs = split_refs(refs, steps, steps, steps, steps)
        gate_out, att_out, gated_out, send_out = outs
        gate = dot_nn(normed_ref[...], rows_of(wg, g_place))
        gate_out[...] = gate
        query = q[...]
        pieces = {}
        for m in range(micros):
            for g in range(kv_heads):
                prob = softmax_of(
                    group_rows(query, m, g), slot_rows(ks, key_place, m, g), qpos[...], kpos[...]
                )
                pieces[m, g] = dot_nn(prob.astype(LOW), slot_rows(vs, value_place, m, g))
        att = ungroup(pieces)
        att_out[...] = att
        gated = (att * jax.nn.sigmoid(gate)).astype(LOW)
        gated_out[...] = gated
        write_blocks(dot_nt(gated, rows_of(wo, o_place)), send_out)

    att_flops = 4 * tokens * total_rows * q_width
    gate_pre, attended, gated_low, send = run_kernel(
        attend_body,
        [
            shape_of((tokens, q_width), F32),
            shape_of((tokens, q_width), F32),
            shape_of((tokens, q_width), LOW),
            block_out,
        ],
        [after(query_low, wire), normed, query_pos, key_pos, *keys, *values, *w_g, *w_o],
        att_flops + 4 * tokens * width * q_width,
    )
    got = exchange_tp(after(send, cot))

    def middle_body(me_ref, x, gain, got_ref, middle_out, low_out, total_ref):
        total_ref[...] = sum_blocks(got_ref)
        rows = x[...] + read_permuted(total_ref, me_ref)
        middle_out[...] = rows
        low = (rows * inverse_rms(rows) * gain[...]).astype(LOW)
        for b in range(p):
            low_out[b] = low

    def run_part(body, outs, args):
        specs = [pl.BlockSpec(memory_space=pltpu.SMEM)]
        specs += [pl.BlockSpec(memory_space=pltpu.VMEM)] * len(args)
        return pl.pallas_call(
            body,
            out_shape=outs,
            in_specs=specs,
            out_specs=[pl.BlockSpec(memory_space=pltpu.VMEM)] * len(outs),
            scratch_shapes=[pltpu.VMEM((ptok, width), F32)],
            compiler_params=pltpu.CompilerParams(vmem_limit_bytes=VMEM_LIMIT),
            cost_estimate=pl.CostEstimate(
                flops=20 * ptok * width, transcendentals=0, bytes_accessed=20 * ptok * width
            ),
        )(me, *args)

    part_f32 = shape_of((ptok, width), F32)
    gain_f32 = shape_of((1, width), F32)
    second = second_gain[None]
    middle, normed_two = run_part(
        middle_body,
        [part_f32, block_out],
        [x_part, second, outer_permute(got)],
    )
    n2 = exchange_tp(normed_two).reshape(tokens, width)
    f_a, fa_place = gather_pieces(f_own[:, :half_a], "seq", go_a, send, n2)
    f_b, fb_place = gather_pieces(f_own[:, half_a:], "seq", go_b, send, n2)

    lanes = n // 2
    halves = (half_a, half_b)
    lane_units = lanes * units
    pair = 2 if lanes % 2 == 0 else 1
    anywhere = pl.BlockSpec(memory_space=pl.ANY)
    whole = pl.BlockSpec(memory_space=pltpu.VMEM)
    f_places = (fa_place, fb_place)

    def start_loads(slots, refs, skipped, w, sem):
        count = len(refs) // 2
        loads = []
        for s, slot in enumerate(slots):
            for t in range(2):
                index, entry = f_places[t][slot]
                where = pl.ds(s * units + t * half_a, halves[t])
                source = refs[t * count + index - skipped].at[entry]
                copy = pltpu.make_async_copy(source, w.at[:, where, :], sem.at[2 * s + t])
                copy.start()
                loads.append(copy)
        return loads

    def pair_rows(step, loads):
        for copy in loads[2 * pair * step : 2 * pair * (step + 1)]:
            copy.wait()
        return slice(step * pair * units, (step + 1) * pair * units)

    def forward_body(last, slots, count, x, *refs):
        held, before, outs, (w, sem) = split_refs(refs, 2 * count, 1 if last else 0, 4)
        loads = start_loads(slots, held, steps - 2 if last else 0, w, sem)
        for step in range(lanes // pair):
            rows = pair_rows(step, loads)
            gate = dot_nt(w[0, rows], x[...])
            up = dot_nt(w[1, rows], x[...])
            outs[0][rows] = gate
            outs[1][rows] = up
            outs[2][rows] = (gate * jax.nn.sigmoid(gate) * up).astype(LOW)
        out = dot_tn(outs[2][...], w[2])
        if last:
            out = out + before[0][...]
        outs[3][...] = out.astype(outs[3].dtype)

    def run_forward(last, dtype, slots, *before):
        use = slice(steps - 2, steps) if last else slice(0, steps - 2)
        held = [*f_a[use], *f_b[use]]
        return pl.pallas_call(
            lambda *r: forward_body(last, slots, len(held) // 2, *r),
            out_shape=[
                shape_of((lane_units, tokens), F32),
                shape_of((lane_units, tokens), F32),
                shape_of((lane_units, tokens), LOW),
                shape_of((tokens, width), dtype),
            ],
            in_specs=[whole] + [anywhere] * len(held) + [whole] * len(before),
            out_specs=[whole] * 4,
            scratch_shapes=[
                pltpu.VMEM((3, lane_units, width), LOW),
                pltpu.SemaphoreType.DMA((2 * lanes,)),
            ],
            compiler_params=pltpu.CompilerParams(vmem_limit_bytes=VMEM_LIMIT),
            cost_estimate=pl.CostEstimate(
                flops=6 * tokens * width * lane_units // 8,
                transcendentals=0,
                bytes_accessed=(6 * lane_units * width + 4 * tokens * width) // 8,
            ),
        )(n2, *held, *before)

    *acts_even, out_even = run_forward(False, F32, even)
    *acts_odd, out_sum = run_forward(True, LOW, odd, out_even)
    out_got = exchange_tp(out_sum.reshape(p, ptok, width))

    def backward_body(first, slots, count, x, c, gate_ref, up_ref, hid_ref, *refs):
        held, before, grads, (acc,), scratch = split_refs(
            refs, 2 * count, 0 if first else 1, 6, 1
        )
        w, low = scratch[:2]
        gbufs, in_sem, out_sem = scratch[2:8], scratch[8], scratch[9]
        loads = start_loads(slots, held, steps - 2 if first else 0, w, in_sem)
        stores = []

        def store(k, step, value):
            t, h = k % 2, halves[k % 2]
            for q in range(pair):
                slot = slots[step * pair + q] & ~1
                start = (lane_a, lane_b)[t].index(slot) * h
                at = pl.ds(start, h)
                source = q * units + t * half_a
                gbufs[k][start : start + h] = value[source : source + h]
                copy = pltpu.make_async_copy(
                    gbufs[k].at[at], grads[k].at[at], out_sem.at[6 * (step * pair + q) + k]
                )
                copy.start()
                stores.append(copy)

        for step in range(lanes // pair):
            rows = pair_rows(step, loads)
            gate, up = gate_ref[rows], up_ref[rows]
            grad = dot_nt(w[2, rows], c[...])
            sig = jax.nn.sigmoid(gate)
            gate_grad = (grad * up * sig * (1.0 + gate * (1.0 - sig))).astype(LOW)
            up_grad = (grad * gate * sig).astype(LOW)
            low[0, rows] = gate_grad
            low[1, rows] = up_grad
            sides = ((hid_ref[rows], c), (gate_grad, x), (up_grad, x))
            for i, (left, right) in zip((2, 0, 1), sides):
                value = dot_nn(left, right[...]).astype(LOW)
                store(2 * i, step, value)
                store(2 * i + 1, step, value)
        back = dot_tn(low[0], w[0]) + dot_tn(low[1], w[1])
        if not first:
            back = back + before[0][...]
        acc[...] = back.astype(acc.dtype)
        for copy in stores:
            copy.wait()

    def run_backward(first, dtype, slots, acts, *before):
        grad_outs = [shape_of((lanes * h, width), LOW) for _ in range(3) for h in halves]
        use = slice(steps - 2, steps) if first else slice(0, steps - 2)
        held = [*f_a[use], *f_b[use]]
        return pl.pallas_call(
            lambda *r: backward_body(first, slots, len(held) // 2, *r),
            out_shape=grad_outs + [shape_of((tokens, width), dtype)],
            in_specs=[whole] * 5 + [anywhere] * len(held) + [whole] * len(before),
            out_specs=[anywhere] * 6 + [whole],
            scratch_shapes=[
                pltpu.VMEM((3, lane_units, width), LOW),
                pltpu.VMEM((2, lane_units, tokens), LOW),
                *[pltpu.VMEM((lanes * h, width), LOW) for _ in range(3) for h in halves],
                pltpu.SemaphoreType.DMA((2 * lanes,)),
                pltpu.SemaphoreType.DMA((6 * lanes,)),
            ],
            compiler_params=pltpu.CompilerParams(vmem_limit_bytes=VMEM_LIMIT),
            cost_estimate=pl.CostEstimate(
                flops=12 * tokens * width * lane_units // 8,
                transcendentals=0,
                bytes_accessed=(12 * lane_units * width + 8 * tokens * width) // 8,
            ),
        )(n2, cot, *acts, *held, *before)

    *f_odd, back_odd = run_backward(True, F32, odd, acts_odd)
    *f_even, back_sum = run_backward(False, LOW, even, acts_even, back_odd)
    back_got = exchange_tp(after(back_sum, out_got).reshape(p, ptok, width))
    orders = (back_a, back_b)

    def first_steps(index):
        return [join_lanes(f_even[2 * index + t], f_odd[2 * index + t]) for t in range(2)]

    def next_steps(states, level, hold=None):
        last = level == len(back_a) - 1
        return [
            scatter_step(state, orders[t][level], last, hold) for t, state in enumerate(states)
        ]

    def last_steps(states, level, hold=None):
        for k in range(level, len(back_a)):
            states = next_steps(states, k, hold)
        return states

    def return_units(states, hold):
        blocks = jnp.concatenate(states).astype(LOW)
        blocks = blocks.reshape(units, p, chunk).transpose(1, 0, 2)
        raw = exchange_tp(after(blocks, hold))
        return raw, raw.reshape(p * units, chunk).astype(F32)

    down, gates, ups = first_steps(2), first_steps(0), first_steps(1)
    down = next_steps(down, 0)

    def branch_body(me_ref, mid, cot_ref, gain, got_ref, mg_out, low_out, gain_out, scratch):
        total = sum_blocks(got_ref)
        rows = mid[...]
        r = inverse_rms(rows)
        unit = rows * r
        gain_out[...] = jnp.sum(total * unit, axis=0, keepdims=True)
        u = total * gain[...]
        grad = cot_ref[...].astype(F32) + r * (u - unit * jnp.mean(u * unit, -1, keepdims=True))
        mg_out[...] = grad
        scratch[...] = grad
        low = read_permuted(scratch, me_ref).astype(LOW)
        for b in range(p):
            low_out[b] = low

    middle_grad, branch_low, grad_second = run_part(
        branch_body,
        [part_f32, block_out, gain_f32],
        [middle, cot_part, second, back_got],
    )
    branch_grad = exchange_tp(outer_permute(branch_low))
    gates = next_steps(gates, 0, branch_low)
    ups = [after(u, *down) for u in ups]
    down_last = last_steps(down, 1, branch_low)
    down_raw, grad_hdown = return_units(down_last, branch_grad)

    def back_body(q, qpre, gate, att, cos, sin, qg, qpos, kpos, *refs):
        ks, vs, wo, (bg,), outs = split_refs(refs, steps, steps, steps, 1)
        k_odd, k_even, v_odd, v_even, dq_out, dg_out, bg_out, gain_out = outs
        branch = read_blocks(bg)
        bg_out[...] = branch
        gated_grad = dot_nn(branch, rows_of(wo, o_place))
        sig = jax.nn.sigmoid(gate[...])
        att_grad = (gated_grad * sig).astype(LOW)
        dg_out[...] = (gated_grad * att[...] * sig * (1.0 - sig)).astype(LOW)
        product = att_grad.astype(F32) * att[...]
        query = q[...]
        pieces = {}
        for m in range(micros):
            for g in range(kv_heads):
                qr = group_rows(query, m, g)
                ag = group_rows(att_grad, m, g)
                key = slot_rows(ks, key_place, m, g)
                value = slot_rows(vs, value_place, m, g)
                delta = jnp.sum(group_rows(product, m, g), axis=-1, keepdims=True)
                prob = softmax_of(qr, key, qpos[...], kpos[...])
                ds = (prob * (dot_nt(ag, value) - delta)).astype(LOW)
                pieces[m, g] = dot_nn(ds, key) * scale
                dk = dot_tn(ds, qr).astype(LOW)
                dv = dot_tn(prob.astype(LOW), ag).astype(LOW)
                for j in range(n):
                    src = slice(j * local_rows, (j + 1) * local_rows)
                    pairs = ((k_odd, k_even, lane_a, dk), (v_odd, v_even, lane_b, dv))
                    for odd_ref, even_ref, lane, value_grad in pairs:
                        dst = lane.index(j & ~1) * tokens + m * local_rows
                        at = (slice(dst, dst + local_rows), slice(g * head, (g + 1) * head))
                        (odd_ref if j % 2 else even_ref)[at] = value_grad[src]
        dq, gain_grad = heads_backward(ungroup(pieces), qpre[...], qg[...], cos[...], sin[...])
        dq_out[...] = dq.astype(LOW)
        gain_out[...] = gain_grad

    lane_kv = shape_of((lanes * tokens, kv_width), LOW)
    k_odd, k_even, v_odd, v_even, dq_low, dg_low, branch_rows, grad_qgain = run_kernel(
        back_body,
        [
            lane_kv,
            lane_kv,
            lane_kv,
            lane_kv,
            shape_of((tokens, q_width), LOW),
            shape_of((tokens, q_width), LOW),
            shape_of((tokens, width), LOW),
            shape_of((1, head), F32),
        ],
        [
            query_low,
            query_pre,
            gate_pre,
            attended,
            cosine,
            sine,
            q_gain,
            query_pos,
            key_pos,
            *keys,
            *values,
            *w_o,
            branch_grad,
        ],
        5 * att_flops // 2 + 2 * tokens * width * q_width,
    )
    key_halves = join_lanes(k_even, k_odd)
    value_halves = join_lanes(v_even, v_odd)
    gates_last = last_steps(gates, 1, (key_halves, value_halves))
    ups_last = last_steps(ups, 0, (key_halves, value_halves))
    key_grad = scatter_lanes(key_halves, back_a, down_raw)
    value_grad = scatter_lanes(value_halves, back_b, down_raw)

    def write_lanes(value, odd_ref, even_ref, lane):
        for j in range(n):
            place = lane.index(j & ~1)
            at = slice(place * block, (place + 1) * block)
            (odd_ref if j % 2 else even_ref)[at] = value[j * block : (j + 1) * block].astype(LOW)

    lane_w = shape_of((lanes * block, q_width), LOW)

    def weight_body(normed_ref, dq, dg, bg, gated, *refs):
        wq, wg, outs = split_refs(refs, steps, steps)
        g_odd, g_even, o_odd, o_even, q_odd, q_even, acc = outs
        low = normed_ref[...]
        write_lanes(dot_tn(low, dg[...]), g_odd, g_even, lane_a)
        write_lanes(dot_tn(bg[...], gated[...]), o_odd, o_even, lane_b)
        write_lanes(dot_tn(low, dq[...]), q_odd, q_even, lane_a)
        acc[...] = dot_nt(dq[...], rows_of(wq, q_place)) + dot_nt(dg[...], rows_of(wg, g_place))

    g_odd, g_even, o_odd, o_even, q_odd, q_even, normed_acc = run_kernel(
        weight_body,
        [lane_w] * 6 + [shape_of((tokens, width), F32)],
        [after(normed, down_raw), dq_low, dg_low, branch_rows, gated_low, *w_q, *w_g],
        10 * tokens * width * q_width,
    )

    def key_body(dk, dv, kpre, cos, sin, kg, normed_ref, acc, *refs):
        wkv, (kv_odd, kv_even, gain_out, send_out) = split_refs(refs, steps)
        dkey, gain_grad = heads_backward(
            dk[...] * scale, kpre[...], kg[...], cos[...], sin[...]
        )
        gain_out[...] = gain_grad
        low = jnp.concatenate([dkey.astype(LOW), dv[...].astype(LOW)], axis=1)
        write_blocks(acc[...] + dot_nt(low, rows_of(wkv, kv_place)), send_out)
        write_lanes(dot_tn(normed_ref[...], low), kv_odd, kv_even, lane_b)

    lane_w2 = shape_of((lanes * block, 2 * kv_width), LOW)
    kv_odd, kv_even, grad_kgain, send = run_kernel(
        key_body,
        [lane_w2, lane_w2, shape_of((1, head), F32), block_out],
        [key_grad, value_grad, key_pre, cosine, sine, k_gain, normed, normed_acc, *w_kv],
        8 * tokens * width * kv_width,
    )
    gate_raw, grad_hgate = return_units(gates_last, down_raw)
    got = exchange_tp(after(send, gate_raw))
    _, grad_hup = return_units(ups_last, got)
    ready = (key_grad, value_grad)
    g_odd, o_odd, q_odd = after((g_odd, o_odd, q_odd), *ready)
    grad_gating = scatter_lanes(join_lanes(g_even, g_odd), back_a)
    grad_outproj = scatter_lanes(join_lanes(o_even, o_odd), back_b, got).T
    grad_query = scatter_lanes(join_lanes(q_even, q_odd), back_a, got)
    grad_kv = scatter_lanes(join_lanes(kv_even, kv_odd), back_b, got)

    def input_body(me_ref, x, gain, mg, got_ref, in_out, gain_out, total_ref):
        total_ref[...] = sum_blocks(got_ref)
        total = read_permuted(total_ref, me_ref)
        rows = x[...]
        r = inverse_rms(rows)
        unit = rows * r
        gain_out[...] = jnp.sum(total * unit, axis=0, keepdims=True)
        u = total * gain[...]
        in_out[...] = mg[...] + r * (u - unit * jnp.mean(u * unit, -1, keepdims=True))

    input_grad, grad_first = run_part(
        input_body,
        [part_f32, gain_f32],
        [x_part, first_gain[None], middle_grad, outer_permute(got)],
    )
    gains = jnp.concatenate([grad_first, grad_second, grad_qgain, grad_kgain], axis=1)
    gains = gains.reshape(-1, head)
    for mask in [1 << b for b in range((p - 1).bit_length())]:
        gains = gains + swap(gains, "tp", mask)
    for mask in masks:
        gains = gains + swap(gains, "seq", mask)
    gains = gains.reshape(-1)

    ffn_out = tree_sum([out_got[b].astype(F32) for b in range(p)])
    layer_rows = (middle + ffn_out).astype(LOW)

    grad_hgate = grad_hgate.T
    grad_hup = grad_hup.T
    return (
        layer_rows.reshape(micros, part, width),
        input_grad.reshape(micros, part, width),
        gains[:width],
        grad_query,
        grad_kv[:, :kv_width],
        grad_kv[:, kv_width:],
        grad_gating,
        grad_outproj,
        gains[2 * width : 2 * width + head],
        gains[2 * width + head :],
        gains[width : 2 * width],
        grad_hgate,
        grad_hup,
        grad_hdown,
    )


def solution(mesh):
    in_specs = (
        P(None, "seq", None),
        P(None, "seq"),
        P(),
        P("seq", "tp"),
        P("seq", "tp"),
        P("seq", "tp"),
        P("seq", "tp"),
        P("tp", "seq"),
        P(),
        P(),
        P(),
        P("tp", "seq"),
        P("tp", "seq"),
        P("seq", "tp"),
        P(None, ("seq", "tp"), None),
    )
    out_specs = (
        P(None, ("seq", "tp"), None),
        P(None, ("seq", "tp"), None),
        P(),
        P("seq", "tp"),
        P("seq", "tp"),
        P("seq", "tp"),
        P("seq", "tp"),
        P("tp", "seq"),
        P(),
        P(),
        P(),
        P("tp", "seq"),
        P("tp", "seq"),
        P("seq", "tp"),
    )
    return jax.shard_map(
        per_device, mesh=mesh, in_specs=in_specs, out_specs=out_specs, check_vma=False
    )
```
